512 devices in a mesh: space: 128 (over z, y, core), dp: 4 (over x).
Axes of the slice: x: 4, y: 4, z: 16, core: 2. Of those that a mesh axis runs over, the one named last changes fastest.
Arguments:
- features: bfloat16 [4, 512, 8, 8, 512], P('dp', 'space'), may hold values from -6 to 6
- occupancy: int32 [4, 512, 512], P('dp', 'space'), may hold values 0 or 1
- counts: int32 [4, 128], P('dp', 'space'), may hold values from 2 to 4, as said below
- send_units: int32 [4, 128, 5, 12], P('dp', 'space'), may hold values from -1 to 23, as said below
- neighbours: int32 [4, 512, 26], P('dp', 'space'), may hold values from -1 to 59, as said below
- weight: bfloat16 [1728, 64], P('dp'), may hold values from -0.15625 to 0.15625
- conv_bias: bfloat16 [64], P('dp'), may hold values from -3 to 3
- cotangent: bfloat16 [4, 512, 8, 8, 512], P('dp', 'space'), may hold values from -6 to 6
Outputs:
- block_output: bfloat16 [4, 512, 8, 8, 512], P('dp', 'space')
- grad_input: bfloat16 [4, 512, 8, 8, 512], P('dp', 'space')
- grad_weight: float32 [1728, 64], P('dp')
- grad_bias: float32 [64], P('dp')
The draws below stay inside these ranges and needn't reach their ends.
Inputs may be any that keep to these rules, and one draw needn't show every extreme that they name: `counts`: each volume has a device holding 4 bricks. `send_units`: the entry of device q at j and l is -1 or 6 times a slot below counts of q plus ((j * 12 + l) mod 6); it is -1 where device q + j - 2 does not exist; link 0 is used wherever that device exists. `neighbours`: an entry n >= 0 of a brick on device r names a unit that device r + 2 - n // 12 sends, whose face is the one the entry's offset needs (2d if o_d = 1, 2d+1 if o_d = -1, d the first dimension where o is not 0).
All inputs are finite; a program needn't handle non-finite values. No bound on the sum of `occupancy` on one device may be relied on, other than what follows from the above.
Results may differ from the reference program's by a relative error of at most 0.012.
Values may be sent and summed in bfloat16 or wider, within the bound.
A program may use at most 64 MiB of HBM per device.

```python
import jax
import jax.numpy as jnp
from jax import lax

C = 64
E = 8
TAPS = 27
SLOTS = 4
REACH = 2
LINKS = 12
VOLS = 4
BRICKS = 512


def neighbour_offsets_drawn():
    return [(first - 1, second - 1, third - 1) for first in range(3) for second in range(3) for third in range(3) if (first, second, third) != (1, 1, 1)]


def needed_face(offset):
    for dimension in range(3):
        if offset[dimension] != 0:
            return 2 * dimension + (0 if offset[dimension] == 1 else 1)
    return 0


def layout(key):
    shards = BRICKS // SLOTS
    spread = 2 * REACH + 1
    base_key = jax.random.fold_in(key, 4242)
    key_list = jax.random.split(base_key, 7)
    counts = jax.random.randint(key_list[0], (VOLS, shards), SLOTS // 2, SLOTS + 1)
    fullest = jax.random.randint(key_list[1], (VOLS, 1), 0, shards)
    counts = jnp.where(jnp.arange(shards)[None, :] == fullest, SLOTS, counts).astype(jnp.int32)
    device = jnp.arange(shards)[None, :, None, None]
    offset = jnp.arange(spread)[None, None, :, None]
    link_id = jnp.arange(LINKS)[None, None, None, :]
    target = device + offset - REACH
    inside = (target >= 0) & (target < shards)
    coin_flip = jax.random.randint(key_list[2], (VOLS, shards, spread, LINKS), 0, 2)
    present = inside & ((link_id == 0) | (coin_flip == 1))
    slot_pick = jax.random.randint(key_list[3], (VOLS, shards, spread, LINKS), 0, SLOTS) % counts[:, :, None, None]
    face_id = (offset * LINKS + link_id) % 6
    send_list = jnp.where(present, slot_pick * 6 + face_id, -1).astype(jnp.int32)
    faces_needed = jnp.array([needed_face(item) for item in neighbour_offsets_drawn()], jnp.int32)
    draw_shape = (VOLS, shards, SLOTS, 26)
    column_pick = jax.random.randint(key_list[5], draw_shape, 0, spread)
    half_pick = jax.random.randint(key_list[6], draw_shape, 0, 2)
    link_pick = faces_needed[None, None, None, :] + 6 * half_pick
    link_pick = jnp.where(link_pick < LINKS, link_pick, faces_needed[None, None, None, :])
    chosen_unit = column_pick * LINKS + link_pick
    source = jnp.arange(shards)[None, :, None, None] + REACH - column_pick
    in_range = (source >= 0) & (source < shards)
    clipped = jnp.clip(source, 0, shards - 1)
    volume_ids = jnp.broadcast_to(jnp.arange(VOLS)[:, None, None, None], draw_shape)
    sent_unit = send_list[volume_ids, clipped, column_pick, link_pick]
    slot_ids = jnp.arange(SLOTS)
    dropped = (jax.random.randint(key_list[4], draw_shape, 0, 4) == 0) & (slot_ids[None, None, :, None] > 0)
    listing = jnp.where(in_range & (sent_unit >= 0) & ~dropped, chosen_unit, -1)
    return (counts, send_list, listing.reshape(VOLS, shards * SLOTS, 26).astype(jnp.int32))


def draw_counts(key, part):
    return layout(key)[0]


def draw_send_units(key, part):
    return layout(key)[1]


def draw_neighbours(key, part):
    return layout(key)[2]


def place_ends(entries, key, low, top_value):
    extent = entries.shape
    spot = [jax.random.randint(jax.random.fold_in(key, axis), (), 0, extent[axis]) for axis in range(len(extent))]
    entries = entries.at[tuple(spot)].set(low)
    longest = extent.index(max(extent))
    spot[longest] = (spot[longest] + 1) % extent[longest]
    return entries.at[tuple(spot)].set(top_value)


def steps_of(own_key, dims, cuts, low, largest):
    def one(dim, shards_of):
        draws = jax.random.uniform(jax.random.fold_in(jax.random.fold_in(own_key, 6), dim), (shards_of,), jnp.float32, low / len(cuts), largest / len(cuts))
        return jnp.repeat(jnp.exp(draws), dims[dim] // shards_of).reshape((-1,) + (1,) * (len(dims) - dim - 1))

    factor_of = one(*cuts[0])
    for cut in cuts[1:]:
        factor_of = factor_of * one(*cut)
    return factor_of


def gaussian(own_key, extent, deviation, most, cuts=(), kind=jnp.bfloat16):
    values = jax.random.normal(own_key, extent, jnp.float32) * deviation
    if len(cuts) > 0:
        values = steps_of(own_key, extent, cuts, -0.22, 0.18) * values
    return jnp.clip(values, min=-most, max=most).astype(kind)


def setup_inputs(seed: int = 0) -> dict:
    seeds = jax.random.split(jax.random.key(seed), 9)
    features = gaussian(seeds[0], (VOLS, BRICKS, E, E, E * C), 1.0, 6.0, ((0, 4), (1, 128)))
    occupancy = place_ends((jax.random.randint(seeds[1], (VOLS, BRICKS, E * E * E), 0, 2) < 1).astype(jnp.int32), jax.random.fold_in(seeds[1], 1), 0, 1)
    counts = draw_counts(jax.random.fold_in(seeds[8], 71), 0)
    send_units = draw_send_units(jax.random.fold_in(seeds[8], 71), 0)
    neighbours = draw_neighbours(jax.random.fold_in(seeds[8], 71), 0)
    weight = gaussian(seeds[5], (TAPS * C, C), (TAPS * C) ** -0.5, 0.15625, ((0, 4),))
    conv_bias = gaussian(seeds[6], (C,), 0.5, 3.0, ((0, 4),))
    cotangent = gaussian(seeds[7], (VOLS, BRICKS, E, E, E * C), 1.0, 6.0, ((0, 4), (1, 128)))
    return dict(features=features, occupancy=occupancy, counts=counts, send_units=send_units, neighbours=neighbours, weight=weight, conv_bias=conv_bias, cotangent=cotangent)


def neighbour_offsets():
    return [(first - 1, second - 1, third - 1) for first in range(3) for second in range(3) for third in range(3) if (first, second, third) != (1, 1, 1)]


def first_moving(offset):
    for dimension in range(3):
        if offset[dimension] != 0:
            return dimension
    return 0


def face_planes(values):
    brick_edge = values.shape[1]
    planes = [values[:, 0], values[:, brick_edge - 1], values[:, :, 0], values[:, :, brick_edge - 1], values[:, :, :, 0], values[:, :, :, brick_edge - 1]]
    return jnp.stack(planes, axis=1)


def rim_region(face_plane, offset, brick_edge):
    moving = first_moving(offset)
    region = face_plane
    other_dims = [dimension for dimension in range(3) if dimension != moving]
    for position, dimension in enumerate(other_dims):
        if offset[dimension] == -1:
            region = lax.slice_in_dim(region, brick_edge - 1, brick_edge, axis=position + 1)
        elif offset[dimension] == 1:
            region = lax.slice_in_dim(region, 0, 1, axis=position + 1)
    return jnp.expand_dims(region, moving + 1)


def halo_block(values, units, listing):
    brick_edge = values.shape[1]
    unit_total = units.shape[0]
    padded = jnp.pad(values, ((0, 0), (1, 1), (1, 1), (1, 1), (0, 0)))
    for offset_index, offset in enumerate(neighbour_offsets()):
        unit_index = listing[:, offset_index]
        face_plane = jnp.take(units, jnp.clip(unit_index, 0, unit_total - 1), axis=0)
        face_plane = face_plane * (unit_index >= 0).astype(face_plane.dtype)[:, None, None, None]
        region = rim_region(face_plane, offset, brick_edge)
        starts = [0] + [0 if step == -1 else (1 if step == 0 else brick_edge + 1) for step in offset] + [0]
        padded = lax.dynamic_update_slice(padded, region, starts)
    return padded


def windows(padded, brick_edge):
    return [padded[:, first:first + brick_edge, second:second + brick_edge, third:third + brick_edge, :] for first in range(3) for second in range(3) for third in range(3)]


def convolve(padded, kernels, brick_edge):
    channels = padded.shape[-1]
    result = jnp.zeros((padded.shape[0] * brick_edge ** 3, kernels.shape[-1]), jnp.float32)
    for tap_index, window in enumerate(windows(padded, brick_edge)):
        result = result + jnp.dot(window.reshape(-1, channels), kernels[tap_index], preferred_element_type=jnp.float32)
    return result.reshape(padded.shape[0], brick_edge, brick_edge, brick_edge, -1)


def weight_terms(padded, grads, brick_edge):
    channels = padded.shape[-1]
    flat_grad = grads.reshape(-1, grads.shape[-1])
    tap_terms = [lax.dot_general(window.reshape(-1, channels), flat_grad, (((0,), (0,)), ((), ())), preferred_element_type=jnp.float32) for window in windows(padded, brick_edge)]
    return jnp.concatenate(tap_terms, axis=0)


def route_units(faces_all, send_list):
    devices = faces_all.shape[0]
    spread = send_list.shape[1]
    link_count = send_list.shape[2]
    reach_span = (spread - 1) // 2
    column = jnp.arange(spread, dtype=jnp.int32)
    source = jnp.arange(devices, dtype=jnp.int32)[:, None] + reach_span - column[None, :]
    inside = (source >= 0) & (source < devices)
    clipped = jnp.clip(source, 0, devices - 1)
    chosen = send_list[clipped[:, :, None], column[None, :, None], jnp.arange(link_count, dtype=jnp.int32)[None, None, :]]
    usable = inside[:, :, None] & (chosen >= 0)
    picked = faces_all[clipped[:, :, None], jnp.clip(chosen, 0, faces_all.shape[1] - 1)]
    picked = picked * usable.astype(picked.dtype)[..., None, None, None]
    return picked.reshape(devices, spread * link_count, picked.shape[3], picked.shape[4], picked.shape[5])


def one_volume(volume_args, kernels, mirrored, bias_row):
    features, occupancy, counts, send_list, neighbours, cotangent = volume_args
    devices = counts.shape[0]
    bricks = features.shape[0]
    slot_count = bricks // devices
    brick_edge = features.shape[1]
    channels = features.shape[3] // brick_edge
    shaped = (devices, slot_count, brick_edge, brick_edge, brick_edge, channels)
    live_slot = (jnp.arange(bricks, dtype=jnp.int32) % slot_count < jnp.repeat(counts, slot_count)).astype(jnp.int32)
    active = (occupancy * live_slot[:, None]).reshape(devices, slot_count, brick_edge, brick_edge, brick_edge, 1)
    masked = features.reshape(shaped) * active.astype(features.dtype)
    listing_all = neighbours.reshape(devices, slot_count, 26)
    grad_all = cotangent.reshape(shaped)

    def faces_of(values):
        return jax.vmap(face_planes)(values).reshape(devices, slot_count * 6, brick_edge, brick_edge, channels)

    units_input = route_units(faces_of(masked), send_list)

    def forward(device_args):
        masked_dev, units_dev, listing, active_dev, grad_dev = device_args
        padded_input = halo_block(masked_dev, units_dev, listing)
        pre_activation = convolve(padded_input, kernels, brick_edge) + bias_row
        sigmoid_pre = jax.nn.sigmoid(pre_activation)
        active_full = active_dev.astype(jnp.float32)
        block_output = (pre_activation * sigmoid_pre * active_full).astype(jnp.bfloat16)
        grad_pre = (grad_dev.astype(jnp.float32) * sigmoid_pre * (1.0 + pre_activation * (1.0 - sigmoid_pre)) * active_full).astype(jnp.bfloat16)
        return block_output, grad_pre

    block_output, grad_pre = lax.map(forward, (masked, units_input, listing_all, active, grad_all))
    units_grad = route_units(faces_of(grad_pre), send_list)

    def backward(carry, device_args):
        masked_dev, units_in_dev, units_grad_dev, listing, active_dev, grad_pre_dev = device_args
        padded_input = halo_block(masked_dev, units_in_dev, listing)
        padded_grad = halo_block(grad_pre_dev, units_grad_dev, listing)
        grad_input = (convolve(padded_grad, mirrored, brick_edge) * active_dev.astype(jnp.float32)).astype(jnp.bfloat16)
        weight_grad = weight_terms(padded_input, grad_pre_dev, brick_edge)
        bias_grad = jnp.sum(grad_pre_dev.astype(jnp.float32).reshape(-1, channels), axis=0)
        return (carry[0] + weight_grad, carry[1] + bias_grad), grad_input

    start_sums = (jnp.zeros((27 * channels, channels), jnp.float32), jnp.zeros((channels,), jnp.float32))
    sums, grad_input = lax.scan(backward, start_sums, (masked, units_input, units_grad, listing_all, active, grad_pre))
    return block_output.reshape(features.shape), grad_input.reshape(features.shape), sums[0], sums[1]


def reference(features, occupancy, counts, send_units, neighbours, weight, conv_bias, cotangent):
    channels = weight.shape[1]
    kernels = weight.reshape(27, channels, channels)
    mirrored = jnp.swapaxes(kernels[::-1], 1, 2)
    bias_row = conv_bias.astype(jnp.float32)

    def per_volume(carry, volume_args):
        block_output, grad_input, weight_grad, bias_grad = one_volume(volume_args, kernels, mirrored, bias_row)
        return (carry[0] + weight_grad, carry[1] + bias_grad), (block_output, grad_input)

    start_sums = (jnp.zeros((27 * channels, channels), jnp.float32), jnp.zeros((channels,), jnp.float32))
    sums, results = lax.scan(per_volume, start_sums, (features, occupancy, counts, send_units, neighbours, cotangent))
    return results[0], results[1], sums[0], sums[1]
```

```python
import jax
import jax.numpy as jnp
from jax import lax
from jax.experimental import pallas as pl
from jax.experimental.pallas import tpu as pltpu
from jax.sharding import PartitionSpec as P

F32 = jnp.float32
BF16 = jnp.bfloat16
MESH = pl.DeviceIdType.MESH
SPACE = 128
DP = 4
GROUP = 8
ZS = 16
COLS = 5
ROWS = 256
LANES = 512
WIDE = 2304
TILES = 14
PACKED = 224
PADDED = 256
PIECE = 32
NEAR = (1, 2, SPACE - 1, SPACE - 2)
XY_LINKS = ((0, 1), (2, 3), (6, 7), (8, 9))


def low_half(shape):
    return lax.broadcasted_iota(jnp.int32, shape, len(shape) - 1) < 64


def near_column(step):
    return {1: 3, 2: 4, SPACE - 1: 1, SPACE - 2: 0}[step]


def swap_halves(v):
    return pltpu.roll(v, 64, axis=v.ndim - 1)


def keep(src, flat, sides, q, values):
    src[q, 0:8] = jnp.zeros((8, 8, 128), F32)
    src[q, 8:40] = values.reshape(32, 8, 128)
    flat[q] = values
    for y in range(2):
        sides[5 * y, :, 128 * q : 128 * q + 128] = jnp.zeros((8, 128), F32)
        for b in range(4):
            rows = pl.ds(64 * b + 7 * y, 8, stride=8)
            sides[5 * y + b + 1, :, 128 * q : 128 * q + 128] = flat[q, rows, :]


def pack_faces(src, sides, snd, out_xy, out_z):
    def slot_of(column, link):
        return ((snd[column, link] + 6) * 43) >> 8

    def plane(column, link):
        slot = slot_of(column, link)
        face = link % 6
        if face >= 2:
            return sides[5 * (face - 2) + slot]
        return jnp.concatenate([src[q, slot * 8 + 7 * face] for q in range(4)], axis=1)

    low = low_half((64, 128))
    for column in range(COLS):
        for q, pair in enumerate(XY_LINKS):
            both = jnp.concatenate([plane(column, link) for link in pair], axis=0)
            out_xy[column, 16 * q : 16 * q + 16, :] = both.astype(BF16)
        for h in range(2):
            first = src[0, pl.ds(slot_of(column, 4 + 6 * h) * 8, 8)].reshape(64, 128)
            last = src[3, pl.ds(slot_of(column, 5 + 6 * h) * 8, 8)].reshape(64, 128)
            both = jnp.where(low, first, last)
            out_z[column, 64 * h : 64 * h + 64, :] = both.astype(BF16)


def face_copies(send_xy, send_z, recv_xy, recv_z, sems):
    me = lax.axis_index("space")
    copies = []
    for n, step in enumerate(NEAR):
        column = near_column(step)
        peer = lax.rem(me + step, SPACE)
        for m, (src, dst) in enumerate(((send_xy, recv_xy), (send_z, recv_z))):
            copies.append(
                pltpu.make_async_remote_copy(
                    src_ref=src.at[column],
                    dst_ref=dst.at[column],
                    send_sem=sems.at[0, 2 * n + m],
                    recv_sem=sems.at[1, 2 * n + m],
                    device_id={"space": peer},
                    device_id_type=MESH,
                )
            )
    return copies


def own_faces(send_xy, send_z, recv_xy, recv_z):
    recv_xy[2] = send_xy[2]
    recv_z[2] = send_z[2]


def first_kernel(
    feat, occ, cnt, snd, w, bias,
    units_xy, units_z, masked, mask, wall,
    ms, flat, sides, send_xy, send_z, wsend, sems, wsems,
):
    me, part = lax.axis_index("space"), lax.axis_index("dp")
    barrier = pltpu.get_barrier_semaphore()
    for step in NEAR:
        pl.semaphore_signal(
            barrier, inc=1, device_id={"space": lax.rem(me + step, SPACE)}, device_id_type=MESH
        )
    for d in range(1, DP):
        pl.semaphore_signal(
            barrier, inc=1, device_id={"dp": lax.rem(part + d, DP)}, device_id_type=MESH
        )

    for m in range(TILES):
        top = w[32 * m : 32 * m + 16, :].astype(F32)
        if m < TILES - 1:
            other = w[32 * m + 16 : 32 * m + 32, :].astype(F32)
        else:
            row = jnp.concatenate([bias[...].astype(F32), jnp.zeros((1, 48), F32)], axis=1)
            first = lax.broadcasted_iota(jnp.int32, (16, 64), 0) == 0
            other = jnp.where(first, jnp.broadcast_to(row, (16, 64)), 0.0)
        wsend[16 * m : 16 * m + 16, :] = jnp.concatenate([top, other], axis=1).astype(BF16)

    place = lax.broadcasted_iota(jnp.int32, (64, LANES), 1)
    owner = (place >> 3) == lax.broadcasted_iota(jnp.int32, (64, LANES), 0)
    spread = []
    for b in range(4):
        live = jnp.minimum(jnp.maximum(cnt[0, 0] - b, 0), 1)
        row = (occ[b : b + 1, :] * live).astype(F32)
        spread.append(jnp.where(owner, jnp.broadcast_to(row, (64, LANES)), 0.0))
    fold = lax.broadcasted_iota(jnp.int32, (LANES, 128), 0) & 7
    fold = (fold == lax.broadcasted_iota(jnp.int32, (LANES, 128), 1)).astype(F32).astype(BF16)
    by_z = jnp.dot(jnp.concatenate(spread, axis=0).astype(BF16), fold, preferred_element_type=F32)
    widen = lax.broadcasted_iota(jnp.int32, (128, LANES), 1) >> 6
    widen = (widen == lax.broadcasted_iota(jnp.int32, (128, LANES), 0)).astype(F32).astype(BF16)
    active = jnp.dot(by_z.astype(BF16), widen, preferred_element_type=F32)
    mask[...] = active.astype(BF16)
    values = feat[...].astype(F32) * active
    for q in range(4):
        keep(ms, flat, sides, q, values[:, 128 * q : 128 * q + 128])
    masked[...] = values.astype(BF16)
    pack_faces(ms, sides, snd, send_xy, send_z)

    pl.semaphore_wait(barrier, len(NEAR) + DP - 1)
    copies = face_copies(send_xy, send_z, units_xy, units_z, sems)
    for d in range(1, DP):
        copies.append(
            pltpu.make_async_remote_copy(
                src_ref=wsend,
                dst_ref=wall.at[part],
                send_sem=wsems.at[0, d],
                recv_sem=wsems.at[1, d],
                device_id={"dp": lax.rem(part + d, DP)},
                device_id_type=MESH,
            )
        )
    for copy in copies:
        copy.start()
    wall[part] = wsend[...]
    own_faces(send_xy, send_z, units_xy, units_z)
    for copy in copies:
        copy.wait()


def read_units(units_xy, units_z, u_xy, u_z):
    for column in range(COLS):
        planes = units_xy[column].astype(F32)
        u_xy[8 * column + 8 : 8 * column + 16] = planes.reshape(8, 8, LANES)
        planes = units_z[column].astype(F32)
        u_z[2 * column + 2 : 2 * column + 4] = planes.reshape(2, 64, 128)


def build_columns(src, nbr, u_xy, u_z, stage, columns):
    low = low_half((8, 128))
    low_row = low_half((1, 128))
    depth = lax.broadcasted_iota(jnp.int32, (8, 640), 0)

    def one_brick(b, carry):
        where_of = {}
        for first in range(3):
            for second in range(3):
                for third in range(3):
                    o = (first - 1, second - 1, third - 1)
                    k = first * 9 + second * 3 + third
                    if k == 13:
                        continue
                    n = nbr[b, k if k < 13 else k - 1] + 12
                    column = (n * 171) >> 11
                    upper = (n - column * 12 + 2) >> 3
                    d = 0 if o[0] else 1 if o[1] else 2
                    face = 2 * d + (0 if o[d] == 1 else 1)
                    if d < 2:
                        where_of[o] = column * 8 + face + 4 * upper
                    else:
                        where_of[o] = column * 2 + upper

        def expand(c):
            t = [c[:, 128 * i : 128 * i + 128] for i in range(5)]
            return jnp.concatenate(
                [
                    t[0], jnp.where(low, t[1], t[4]),
                    t[1], jnp.where(low, t[2], t[0]),
                    t[2], jnp.where(low, t[3], t[1]),
                    t[3], jnp.where(low, t[4], t[2]),
                ],
                axis=1,
            )

        def side_row(ox, oy, row):
            rows = slice(row, row + 1)
            middle = u_xy[where_of[ox, oy, 0], rows, :]
            after = u_xy[where_of[ox, oy, 1], rows, 0:128]
            before = u_xy[where_of[ox, oy, -1], rows, 384:512]
            return jnp.concatenate([middle, jnp.where(low_row, after, before)], axis=1)

        for xx in range(10):
            if 1 <= xx <= 8:
                here = jnp.concatenate([src[q, b * 8 + 7 + xx] for q in range(4)], axis=1)
                rows = slice(8 * xx - 8, 8 * xx)
                after = u_z[where_of[0, 0, 1], rows, :]
                before = u_z[where_of[0, 0, -1], rows, :]
                lower, upper = side_row(0, -1, xx - 1), side_row(0, 1, xx - 1)
            else:
                ox = -1 if xx == 0 else 1
                here = u_xy[where_of[ox, 0, 0]]
                after = u_xy[where_of[ox, 0, 1], :, 0:128]
                before = u_xy[where_of[ox, 0, -1], :, 384:512]
                lower, upper = side_row(ox, -1, 7), side_row(ox, 1, 0)
            c = jnp.concatenate([here, jnp.where(low, after, before)], axis=1)
            down = jnp.where(depth == 0, jnp.broadcast_to(lower, (8, 640)), pltpu.roll(c, 1, axis=0))
            up = jnp.where(depth == 7, jnp.broadcast_to(upper, (8, 640)), pltpu.roll(c, 7, axis=0))
            for e, tile in enumerate((down, c, up)):
                stage[e, 8 * xx : 8 * xx + 8, :] = expand(tile)
        for a in range(3):
            for e in range(3):
                t = 3 * a + e
                for p in range(4):
                    rows = pl.ds(pl.multiple_of(b * 64, 64) + 256 * p, 64)
                    columns[rows, 256 * t : 256 * t + 256] = stage[
                        e, 8 * a : 8 * a + 64, 256 * p : 256 * p + 256
                    ].astype(BF16)
        return carry

    lax.fori_loop(0, 4, one_brick, 0)


def build_bands(wall, both, forward, backward):
    low = low_half((16, 128))
    for i in range(DP):
        for m in range(TILES):
            tile = wall[i, 16 * m : 16 * m + 16, :].astype(F32)
            turned = swap_halves(tile)
            row = 16 * (27 * i + 2 * m)
            both[row : row + 16, :] = jnp.where(low, tile, turned)
            if m < TILES - 1:
                both[row + 16 : row + 32, :] = jnp.where(low, turned, tile)
    low = low_half((64, 128))
    for t in range(9):
        w0, w1, w2 = (both[64 * (3 * t + f) : 64 * (3 * t + f) + 64, :] for f in range(3))
        parts = [
            jnp.where(low, w1, w0),
            jnp.where(low, w2, w1),
            jnp.where(low, 0.0, w2),
            jnp.where(low, w0, 0.0),
        ]
        for n, part in enumerate(parts):
            part = part.astype(BF16)
            row = 256 * t + 64 * n
            forward[row : row + 64, :] = part
            lane = 256 * (8 - t) + 128 * (n // 2)
            row = 64 * (n % 2)
            backward[row : row + 64, lane : lane + 128] = part


def whole_bias(wall):
    lane = lax.broadcasted_iota(jnp.int32, (16, 128), 1)
    total = jnp.zeros((16, 128), F32)
    for i in range(DP):
        tile = wall[i, PACKED - 16 : PACKED, :].astype(F32)
        tile = jnp.where((lane >= 64) & (lane < 80), tile, 0.0)
        total += pltpu.roll(tile, 64 + 16 * i, axis=1)
        total += pltpu.roll(tile, 16 * i, axis=1) if i else tile
    return total[0:1, :]


def second_kernel(
    masked, mask, cot, units_xy, units_z, wall, nbr, snd,
    block_out, grad_in, gw, gb,
    src, u_xy, u_z, stage, columns, both, forward, backward,
    grad, flat, sides, send_xy, send_z, recv_xy, recv_z, turned,
    sums, packed, dp_recv, dp_sum, y_recv, z_recv, full,
    sems, dp_sems, y_sems, z_sems, ag_sems,
):
    me, part = lax.axis_index("space"), lax.axis_index("dp")
    zed, spot = me // GROUP, lax.rem(me, GROUP)
    barrier = pltpu.get_barrier_semaphore()

    def in_group(d):
        return {"space": zed * GROUP + lax.rem(spot + d, GROUP)}

    def along_z(d):
        return {"space": lax.rem(zed + d, ZS) * GROUP + spot}

    def along_dp(d):
        return {"dp": lax.rem(part + d, DP)}

    peers = [along_z(d) for d in range(1, ZS)]
    peers += [{"space": lax.rem(me + step, SPACE)} for step in NEAR]
    peers += [along_dp(d) for d in range(1, DP)] + [in_group(d) for d in range(1, GROUP)]
    for peer in peers:
        pl.semaphore_signal(barrier, inc=1, device_id=peer, device_id_type=MESH)

    u_xy[0:8] = jnp.zeros((8, 8, LANES), F32)
    u_z[0:2] = jnp.zeros((2, 64, 128), F32)
    build_bands(wall, both, forward, backward)
    read_units(units_xy, units_z, u_xy, u_z)
    for q in range(4):
        values = masked[:, 128 * q : 128 * q + 128].astype(F32)
        src[q, 8:40] = values.reshape(32, 8, 128)
    build_columns(src, nbr, u_xy, u_z, stage, columns)

    bias = whole_bias(wall)
    bias_sum = jnp.zeros((1, 128), F32)
    for p in range(4):
        lanes = slice(128 * p, 128 * p + 128)
        pre = jnp.dot(
            columns[256 * p : 256 * p + 256, :], forward[...], preferred_element_type=F32
        )
        pre = pre + bias
        sig = jax.nn.sigmoid(pre)
        on = mask[:, lanes].astype(F32)
        block_out[:, lanes] = (pre * sig * on).astype(BF16)
        g = cot[:, lanes].astype(F32) * sig * (1.0 + pre * (1.0 - sig)) * on
        g = g.astype(BF16).astype(F32)
        keep(grad, flat, sides, p, g)
        turned[:, 256 * p : 256 * p + 256] = g.T.astype(BF16)
        bias_sum += jnp.sum(g, axis=0, keepdims=True)
    pack_faces(grad, sides, snd, send_xy, send_z)

    pl.semaphore_wait(barrier, len(peers))
    face = face_copies(send_xy, send_z, recv_xy, recv_z, sems)
    for copy in face:
        copy.start()
    own_faces(send_xy, send_z, recv_xy, recv_z)

    for t in range(9):
        r = jnp.dot(
            turned[...], columns[:, 256 * t : 256 * t + 256], preferred_element_type=F32
        ).T
        r0, r1, r2, r3 = (r[64 * n : 64 * n + 64, :] for n in range(4))
        row = 192 * t
        sums[row : row + 64, :] = r3 + swap_halves(r0)
        sums[row + 64 : row + 128, :] = r0 + swap_halves(r1)
        sums[row + 128 : row + 192, :] = r1 + swap_halves(r2)
    low = low_half((16, 128))
    top_row = lax.broadcasted_iota(jnp.int32, (16, 128), 0) == 0
    bias_sum = bias_sum + swap_halves(bias_sum)
    bias_tile = jnp.where(top_row, jnp.broadcast_to(bias_sum, (16, 128)), 0.0)
    for i in range(DP):
        for m in range(TILES):
            row = 16 * (27 * i + 2 * m)
            if m < TILES - 1:
                other = swap_halves(sums[row + 16 : row + 32, :])
            else:
                other = bias_tile
            tile = jnp.where(low, sums[row : row + 16, :], other)
            packed[i, 16 * m : 16 * m + 16, :] = tile.astype(BF16)
        packed[i, PACKED:PADDED, :] = jnp.zeros((PADDED - PACKED, 128), BF16)

    dp_copies = [
        pltpu.make_async_remote_copy(
            src_ref=packed.at[lax.rem(part + d, DP)],
            dst_ref=dp_recv.at[d - 1],
            send_sem=dp_sems.at[0, d],
            recv_sem=dp_sems.at[1, d],
            device_id=along_dp(d),
            device_id_type=MESH,
        )
        for d in range(1, DP)
    ]
    for copy in dp_copies:
        copy.start()

    for copy in face:
        copy.wait()
    read_units(recv_xy, recv_z, u_xy, u_z)
    build_columns(grad, nbr, u_xy, u_z, stage, columns)

    def grad_input(p):
        lanes = slice(128 * p, 128 * p + 128)
        r = lax.dot_general(
            columns[256 * p : 256 * p + 256, :],
            backward[...],
            (((1,), (1,)), ((), ())),
            preferred_element_type=F32,
        )
        grad_in[:, lanes] = (r * mask[:, lanes].astype(F32)).astype(BF16)

    for copy in dp_copies:
        copy.wait()
    total = packed[part].astype(F32)
    for d in range(DP - 1):
        total += dp_recv[d].astype(F32)
    dp_sum[...] = total.astype(BF16)
    y_copies = [
        pltpu.make_async_remote_copy(
            src_ref=dp_sum.at[pl.ds(pl.multiple_of(lax.rem(spot + d, GROUP) * PIECE, PIECE), PIECE)],
            dst_ref=y_recv.at[d - 1],
            send_sem=y_sems.at[0, d],
            recv_sem=y_sems.at[1, d],
            device_id=in_group(d),
            device_id_type=MESH,
        )
        for d in range(1, GROUP)
    ]
    for copy in y_copies:
        copy.start()
    grad_input(0)
    grad_input(1)

    for copy in y_copies:
        copy.wait()
    mine = pl.ds(pl.multiple_of(spot * PIECE, PIECE), PIECE)
    total = dp_sum[mine, :].astype(F32)
    for d in range(GROUP - 1):
        total += y_recv[d].astype(F32)
    z_recv[zed] = total.astype(BF16)
    z_copies = [
        pltpu.make_async_remote_copy(
            src_ref=z_recv.at[zed],
            dst_ref=z_recv.at[zed],
            send_sem=z_sems.at[0, d],
            recv_sem=z_sems.at[1, d],
            device_id=along_z(d),
            device_id_type=MESH,
        )
        for d in (8, 7, 9, 6, 10, 5, 11, 4, 12, 3, 13, 2, 14, 1, 15)
    ]
    for copy in z_copies:
        copy.start()
    grad_input(2)
    grad_input(3)

    for copy in z_copies:
        copy.wait()
    total = z_recv[0].astype(F32)
    for d in range(1, ZS):
        total += z_recv[d].astype(F32)
    full[mine, :] = total.astype(BF16)
    ag_copies = [
        pltpu.make_async_remote_copy(
            src_ref=full.at[mine],
            dst_ref=full.at[mine],
            send_sem=ag_sems.at[0, d],
            recv_sem=ag_sems.at[1, d],
            device_id=in_group(d),
            device_id_type=MESH,
        )
        for d in range(1, GROUP)
    ]
    for copy in ag_copies:
        copy.start()
    for copy in ag_copies:
        copy.wait()

    for m in range(TILES):
        tile = full[16 * m : 16 * m + 16, :].astype(F32)
        other = swap_halves(tile)
        gw[32 * m : 32 * m + 16, :] = tile[:, 0:64]
        if m < TILES - 1:
            gw[32 * m + 16 : 32 * m + 32, :] = other[:, 0:64]
        else:
            picked = jnp.zeros((16, 128), F32)
            for i in range(DP):
                turn = pltpu.roll(other, 128 - 16 * i, axis=1) if i else other
                picked = jnp.where(part == i, turn, picked)
            gb[...] = picked[0:1, 0:16]


def vmem(n):
    return [pl.BlockSpec(memory_space=pltpu.VMEM)] * n


def smem(n):
    return [pl.BlockSpec(memory_space=pltpu.SMEM)] * n


def of(shape, dtype):
    return jax.ShapeDtypeStruct(shape, dtype)


def body(features, occupancy, counts, send_units, neighbours, weight, conv_bias, cotangent):
    shard_shape = features.shape
    sends = send_units[0, 0]
    units_xy, units_z, masked, mask, wall = pl.pallas_call(
        first_kernel,
        out_shape=(
            of((COLS, 64, LANES), BF16),
            of((COLS, 128, 128), BF16),
            of((ROWS, LANES), BF16),
            of((ROWS, LANES), BF16),
            of((DP, PACKED, 128), BF16),
        ),
        in_specs=vmem(2) + smem(2) + vmem(2),
        out_specs=tuple(vmem(5)),
        scratch_shapes=[
            pltpu.VMEM((4, 40, 8, 128), F32),
            pltpu.VMEM((4, ROWS, 128), F32),
            pltpu.VMEM((10, 8, LANES), F32),
            pltpu.VMEM((COLS, 64, LANES), BF16),
            pltpu.VMEM((COLS, 128, 128), BF16),
            pltpu.VMEM((PACKED, 128), BF16),
            pltpu.SemaphoreType.DMA((2, 8)),
            pltpu.SemaphoreType.DMA((2, DP)),
        ],
        compiler_params=pltpu.CompilerParams(collective_id=0, has_side_effects=True),
        name="trade_faces",
    )(
        features.reshape(ROWS, LANES), occupancy[0], counts, sends, weight, conv_bias.reshape(1, 16)
    )
    block_out, grad_in, gw, gb = pl.pallas_call(
        second_kernel,
        out_shape=(
            of((ROWS, LANES), BF16),
            of((ROWS, LANES), BF16),
            of((432, 64), F32),
            of((1, 16), F32),
        ),
        in_specs=vmem(6) + smem(2),
        out_specs=tuple(vmem(4)),
        scratch_shapes=[
            pltpu.VMEM((4, 40, 8, 128), F32),
            pltpu.VMEM((48, 8, LANES), F32),
            pltpu.VMEM((12, 64, 128), F32),
            pltpu.VMEM((3, 80, 1024), F32),
            pltpu.VMEM((1024, WIDE), BF16),
            pltpu.VMEM((1728, 128), F32),
            pltpu.VMEM((WIDE, 128), BF16),
            pltpu.VMEM((128, WIDE), BF16),
            pltpu.VMEM((4, 40, 8, 128), F32),
            pltpu.VMEM((4, ROWS, 128), F32),
            pltpu.VMEM((10, 8, LANES), F32),
            pltpu.VMEM((COLS, 64, LANES), BF16),
            pltpu.VMEM((COLS, 128, 128), BF16),
            pltpu.VMEM((COLS, 64, LANES), BF16),
            pltpu.VMEM((COLS, 128, 128), BF16),
            pltpu.VMEM((128, 1024), BF16),
            pltpu.VMEM((1728, 128), F32),
            pltpu.VMEM((DP, PADDED, 128), BF16),
            pltpu.VMEM((DP - 1, PADDED, 128), BF16),
            pltpu.VMEM((PADDED, 128), BF16),
            pltpu.VMEM((GROUP - 1, PIECE, 128), BF16),
            pltpu.VMEM((ZS, PIECE, 128), BF16),
            pltpu.VMEM((PADDED, 128), BF16),
            pltpu.SemaphoreType.DMA((2, 8)),
            pltpu.SemaphoreType.DMA((2, DP)),
            pltpu.SemaphoreType.DMA((2, GROUP)),
            pltpu.SemaphoreType.DMA((2, ZS)),
            pltpu.SemaphoreType.DMA((2, GROUP)),
        ],
        compiler_params=pltpu.CompilerParams(
            collective_id=1, has_side_effects=True, vmem_limit_bytes=60 * 1024 * 1024
        ),
        name="convolve_and_reduce",
    )(
        masked, mask, cotangent.reshape(ROWS, LANES), units_xy, units_z, wall, neighbours[0], sends
    )
    return block_out.reshape(shard_shape), grad_in.reshape(shard_shape), gw, gb.reshape(16)


def solution(mesh):
    placed = (
        P("dp", "space", None, None, None),
        P("dp", "space", None),
        P("dp", "space"),
        P("dp", "space", None, None),
        P("dp", "space", None),
        P("dp", None),
        P("dp"),
        P("dp", "space", None, None, None),
    )
    return jax.shard_map(
        body,
        mesh=mesh,
        in_specs=placed,
        out_specs=(
            P("dp", "space", None, None, None),
            P("dp", "space", None, None, None),
            P("dp", None),
            P("dp"),
        ),
        check_vma=False,
    )
```

```python
import jax
import jax.numpy as jnp
from jax import lax
from jax.experimental import pallas as pl
from jax.experimental.pallas import tpu as pltpu
from jax.sharding import PartitionSpec as P

F32 = jnp.float32
BF16 = jnp.bfloat16
MESH = pl.DeviceIdType.MESH
SPACE = 128
DP = 4
GROUP = 8
ZS = 16
COLS = 5
ROWS = 256
LANES = 512
WIDE = 2304
TILES = 14
PACKED = 224
PADDED = 256
PIECE = 32
NEAR = (1, 2, SPACE - 1, SPACE - 2)
RS_ORDER = [(dx, dg) for dx in (2, 1, 3, 0) for dg in (4, 5, 3, 2, 6, 7, 1, 0) if (dx, dg) != (0, 0)]
XY_LINKS = ((0, 1), (2, 3), (6, 7), (8, 9))


def low_half(shape):
    return lax.broadcasted_iota(jnp.int32, shape, len(shape) - 1) < 64


def near_column(step):
    return {1: 3, 2: 4, SPACE - 1: 1, SPACE - 2: 0}[step]


def swap_halves(v):
    return pltpu.roll(v, 64, axis=v.ndim - 1)


def keep(src, flat, sides, q, values):
    src[q, 0:8] = jnp.zeros((8, 8, 128), F32)
    src[q, 8:40] = values.reshape(32, 8, 128)
    flat[q] = values
    for y in range(2):
        sides[5 * y, :, 128 * q : 128 * q + 128] = jnp.zeros((8, 128), F32)
        for b in range(4):
            rows = pl.ds(64 * b + 7 * y, 8, stride=8)
            sides[5 * y + b + 1, :, 128 * q : 128 * q + 128] = flat[q, rows, :]


def pack_faces(src, sides, snd, out_xy, out_z):
    def slot_of(column, link):
        return ((snd[column, 0, link] + 6) * 43) >> 8

    def plane(column, link):
        slot = slot_of(column, link)
        face = link % 6
        if face >= 2:
            return sides[5 * (face - 2) + slot]
        return jnp.concatenate([src[q, slot * 8 + 7 * face] for q in range(4)], axis=1)

    low = low_half((64, 128))
    for column in range(COLS):
        for q, pair in enumerate(XY_LINKS):
            both = jnp.concatenate([plane(column, link) for link in pair], axis=0)
            out_xy[column, 16 * q : 16 * q + 16, :] = both.astype(BF16)
        for h in range(2):
            first = src[0, pl.ds(slot_of(column, 4 + 6 * h) * 8, 8)].reshape(64, 128)
            last = src[3, pl.ds(slot_of(column, 5 + 6 * h) * 8, 8)].reshape(64, 128)
            both = jnp.where(low, first, last)
            out_z[column, 64 * h : 64 * h + 64, :] = both.astype(BF16)


def face_copies(send_xy, send_z, recv_xy, recv_z, sems):
    me = lax.axis_index("space")
    copies = []
    for n, step in enumerate(NEAR):
        column = near_column(step)
        peer = lax.rem(me + step, SPACE)
        for m, (src, dst) in enumerate(((send_xy, recv_xy), (send_z, recv_z))):
            copies.append(
                pltpu.make_async_remote_copy(
                    src_ref=src.at[column],
                    dst_ref=dst.at[column],
                    send_sem=sems.at[0, 2 * n + m],
                    recv_sem=sems.at[1, 2 * n + m],
                    device_id={"space": peer},
                    device_id_type=MESH,
                )
            )
    return copies


def own_faces(send_xy, send_z, recv_xy, recv_z):
    recv_xy[2] = send_xy[2]
    recv_z[2] = send_z[2]


def pack_weights(wt, bias, wsend):
    row = jnp.concatenate([bias[...].astype(F32), jnp.zeros((1, 48), F32)], axis=1)
    first = lax.broadcasted_iota(jnp.int32, (16, 64), 0) == 0
    last = jnp.where(first, jnp.broadcast_to(row, (16, 64)), 0.0)
    for n in range(4):
        if n < 3:
            tile = wt[:, 128 * n : 128 * n + 128].astype(F32)
        else:
            tile = jnp.concatenate([wt[:, 384:432].astype(F32), jnp.zeros((64, 80), F32)], axis=1)
        tile = tile.T
        for m in range(4 if n < 3 else 2):
            other = tile[32 * m + 16 : 32 * m + 32] if 4 * n + m < TILES - 1 else last
            both = jnp.concatenate([tile[32 * m : 32 * m + 16], other], axis=1)
            wsend[64 * n + 16 * m : 64 * n + 16 * m + 16, :] = both.astype(BF16)


def expand_mask(occ, cnt):
    place = lax.broadcasted_iota(jnp.int32, (64, LANES), 1)
    owner = (place >> 3) == lax.broadcasted_iota(jnp.int32, (64, LANES), 0)
    spread = []
    for b in range(4):
        live = jnp.minimum(jnp.maximum(cnt[0, 0] - b, 0), 1)
        row = (occ[b : b + 1, :] * live).astype(F32)
        spread.append(jnp.where(owner, jnp.broadcast_to(row, (64, LANES)), 0.0))
    fold = lax.broadcasted_iota(jnp.int32, (LANES, 128), 0) & 7
    fold = (fold == lax.broadcasted_iota(jnp.int32, (LANES, 128), 1)).astype(F32).astype(BF16)
    by_z = jnp.dot(jnp.concatenate(spread, axis=0).astype(BF16), fold, preferred_element_type=F32)
    widen = lax.broadcasted_iota(jnp.int32, (128, LANES), 1) >> 6
    widen = (widen == lax.broadcasted_iota(jnp.int32, (128, LANES), 0)).astype(F32).astype(BF16)
    return jnp.dot(by_z.astype(BF16), widen, preferred_element_type=F32)


def read_units(units_xy, units_z, u_xy, u_z):
    for column in range(COLS):
        planes = units_xy[column].astype(F32)
        u_xy[8 * column + 8 : 8 * column + 16] = planes.reshape(8, 8, LANES)
        planes = units_z[column].astype(F32)
        u_z[2 * column + 2 : 2 * column + 4] = planes.reshape(2, 64, 128)


def build_columns(src, nbr, u_xy, u_z, stage, columns):
    low = low_half((8, 128))
    low_row = low_half((1, 128))
    depth = lax.broadcasted_iota(jnp.int32, (8, 640), 0)

    def one_brick(b, carry):
        where_of = {}
        for first in range(3):
            for second in range(3):
                for third in range(3):
                    o = (first - 1, second - 1, third - 1)
                    k = first * 9 + second * 3 + third
                    if k == 13:
                        continue
                    n = nbr[b, k if k < 13 else k - 1] + 12
                    column = (n * 171) >> 11
                    upper = (n - column * 12 + 2) >> 3
                    d = 0 if o[0] else 1 if o[1] else 2
                    face = 2 * d + (0 if o[d] == 1 else 1)
                    if d < 2:
                        where_of[o] = column * 8 + face + 4 * upper
                    else:
                        where_of[o] = column * 2 + upper

        def expand(c):
            t = [c[:, 128 * i : 128 * i + 128] for i in range(5)]
            return jnp.concatenate(
                [
                    t[0], jnp.where(low, t[1], t[4]),
                    t[1], jnp.where(low, t[2], t[0]),
                    t[2], jnp.where(low, t[3], t[1]),
                    t[3], jnp.where(low, t[4], t[2]),
                ],
                axis=1,
            )

        def side_row(ox, oy, row):
            rows = slice(row, row + 1)
            middle = u_xy[where_of[ox, oy, 0], rows, :]
            after = u_xy[where_of[ox, oy, 1], rows, 0:128]
            before = u_xy[where_of[ox, oy, -1], rows, 384:512]
            return jnp.concatenate([middle, jnp.where(low_row, after, before)], axis=1)

        for xx in range(10):
            if 1 <= xx <= 8:
                here = jnp.concatenate([src[q, b * 8 + 7 + xx] for q in range(4)], axis=1)
                rows = slice(8 * xx - 8, 8 * xx)
                after = u_z[where_of[0, 0, 1], rows, :]
                before = u_z[where_of[0, 0, -1], rows, :]
                lower, upper = side_row(0, -1, xx - 1), side_row(0, 1, xx - 1)
            else:
                ox = -1 if xx == 0 else 1
                here = u_xy[where_of[ox, 0, 0]]
                after = u_xy[where_of[ox, 0, 1], :, 0:128]
                before = u_xy[where_of[ox, 0, -1], :, 384:512]
                lower, upper = side_row(ox, -1, 7), side_row(ox, 1, 0)
            c = jnp.concatenate([here, jnp.where(low, after, before)], axis=1)
            down = jnp.where(depth == 0, jnp.broadcast_to(lower, (8, 640)), pltpu.roll(c, 1, axis=0))
            up = jnp.where(depth == 7, jnp.broadcast_to(upper, (8, 640)), pltpu.roll(c, 7, axis=0))
            for e, tile in enumerate((down, c, up)):
                stage[e, 8 * xx : 8 * xx + 8, :] = expand(tile)
        for a in range(3):
            for e in range(3):
                t = 3 * a + e
                for p in range(4):
                    rows = pl.ds(pl.multiple_of(b * 64, 64) + 256 * p, 64)
                    columns[rows, 256 * t : 256 * t + 256] = stage[
                        e, 8 * a : 8 * a + 64, 256 * p : 256 * p + 256
                    ].astype(BF16)
        return carry

    lax.fori_loop(0, 4, one_brick, 0)


def build_bands(wall, both, forward, backward):
    low = low_half((16, 128))
    for i in range(DP):
        for m in range(TILES):
            tile = wall[i, 16 * m : 16 * m + 16, :].astype(F32)
            turned = swap_halves(tile)
            row = 16 * (27 * i + 2 * m)
            both[row : row + 16, :] = jnp.where(low, tile, turned)
            if m < TILES - 1:
                both[row + 16 : row + 32, :] = jnp.where(low, turned, tile)
    low = low_half((64, 128))
    for t in range(9):
        w0, w1, w2 = (both[64 * (3 * t + f) : 64 * (3 * t + f) + 64, :] for f in range(3))
        parts = [
            jnp.where(low, w1, w0),
            jnp.where(low, w2, w1),
            jnp.where(low, 0.0, w2),
            jnp.where(low, w0, 0.0),
        ]
        for n, part in enumerate(parts):
            part = part.astype(BF16)
            row = 256 * t + 64 * n
            forward[row : row + 64, :] = part
            lane = 256 * (8 - t) + 128 * (n // 2)
            row = 64 * (n % 2)
            backward[row : row + 64, lane : lane + 128] = part


def whole_bias(wall):
    lane = lax.broadcasted_iota(jnp.int32, (16, 128), 1)
    total = jnp.zeros((16, 128), F32)
    for i in range(DP):
        tile = wall[i, PACKED - 16 : PACKED, :].astype(F32)
        tile = jnp.where((lane >= 64) & (lane < 80), tile, 0.0)
        total += pltpu.roll(tile, 64 + 16 * i, axis=1)
        total += pltpu.roll(tile, 16 * i, axis=1) if i else tile
    return total[0:1, :]


def main_kernel(
    cnt, feat, occ, wt, bias, cot, snd_in, nbr_in,
    block_out, grad_in, full,
    snd, nbr, feat_v, occ_v, wt_v, bias_v, cot_v, mask, wsend, wall,
    src, u_xy, u_z, stage, columns, both, forward, backward,
    flat, sides, send_xy, send_z, recv_xy, recv_z, send_gxy, send_gz, recv_gxy, recv_gz, turned,
    sums, packed, rs_recv, z_recv,
    in_sems, sems, gsems, wsems, rs_sems, z_sems, ag_sems, ready,
):
    me, part = lax.axis_index("space"), lax.axis_index("dp")
    zed, spot = me // GROUP, lax.rem(me, GROUP)
    barrier = pltpu.get_barrier_semaphore()

    def in_group(d):
        return {"space": zed * GROUP + lax.rem(spot + d, GROUP)}

    def along_z(d):
        return {"space": lax.rem(zed + d, ZS) * GROUP + spot}

    def along_dp(d):
        return {"dp": lax.rem(part + d, DP)}

    def tell(sem, peers):
        for peer in peers:
            pl.semaphore_signal(sem, inc=1, device_id=peer, device_id_type=MESH)

    across = [along_dp(d) for d in range(1, DP)]
    beside = [along_z(1), along_z(ZS - 1)]
    near = [{"space": lax.rem(me + step, SPACE)} for step in NEAR]
    near += across + beside + [in_group(d) for d in range(1, GROUP)]
    tell(barrier, near)
    loads = [
        pltpu.make_async_copy(far, here, in_sems.at[n])
        for n, (far, here) in enumerate(
            (
                (occ, occ_v), (feat, feat_v), (wt, wt_v), (bias, bias_v), (cot, cot_v),
                (snd_in, snd), (nbr_in, nbr),
            )
        )
    ]
    for load in loads:
        load.start()

    loads[0].wait()
    active = expand_mask(occ_v, cnt)
    mask[...] = active.astype(BF16)
    loads[1].wait()
    values = feat_v[...].astype(F32) * active
    for q in range(4):
        keep(src, flat, sides, q, values[:, 128 * q : 128 * q + 128])
    loads[5].wait()
    pack_faces(src, sides, snd, send_xy, send_z)
    loads[2].wait()
    loads[3].wait()
    pack_weights(wt_v, bias_v, wsend)

    pl.semaphore_wait(barrier, len(near))
    copies = face_copies(send_xy, send_z, recv_xy, recv_z, sems)
    shares = [
        pltpu.make_async_remote_copy(
            src_ref=wsend,
            dst_ref=wall.at[part],
            send_sem=wsems.at[0, d],
            recv_sem=wsems.at[1, d],
            device_id=along_dp(d),
            device_id_type=MESH,
        )
        for d in range(1, DP)
    ]
    for copy in copies + shares:
        copy.start()
    tell(ready.at[0], across + beside)
    wall[part] = wsend[...]
    own_faces(send_xy, send_z, recv_xy, recv_z)
    u_xy[0:8] = jnp.zeros((8, 8, LANES), F32)
    u_z[0:2] = jnp.zeros((2, 64, 128), F32)
    for copy in shares:
        copy.wait()
    build_bands(wall, both, forward, backward)
    bias_row = whole_bias(wall)
    for copy in copies:
        copy.wait()
    pl.semaphore_wait(ready.at[0], len(across) + len(beside))
    tell(ready.at[1], [along_z(2), along_z(ZS - 2)])

    loads[6].wait()
    read_units(recv_xy, recv_z, u_xy, u_z)
    build_columns(src, nbr, u_xy, u_z, stage, columns)
    loads[4].wait()
    bias_sum = jnp.zeros((1, 128), F32)
    for p in range(4):
        lanes = slice(128 * p, 128 * p + 128)
        pre = jnp.dot(
            columns[256 * p : 256 * p + 256, :], forward[...], preferred_element_type=F32
        )
        pre = pre + bias_row
        sig = jax.nn.sigmoid(pre)
        on = mask[:, lanes].astype(F32)
        block_out[:, lanes] = (pre * sig * on).astype(BF16)
        g = cot_v[:, lanes].astype(F32) * sig * (1.0 + pre * (1.0 - sig)) * on
        g = g.astype(BF16).astype(F32)
        keep(src, flat, sides, p, g)
        turned[:, 256 * p : 256 * p + 256] = g.T.astype(BF16)
        bias_sum += jnp.sum(g, axis=0, keepdims=True)
    pack_faces(src, sides, snd, send_gxy, send_gz)

    face = face_copies(send_gxy, send_gz, recv_gxy, recv_gz, gsems)
    for copy in face:
        copy.start()
    own_faces(send_gxy, send_gz, recv_gxy, recv_gz)
    pl.semaphore_wait(ready.at[1], 2)
    tell(ready.at[2], [along_z(4), along_z(ZS - 4)])

    for t in range(9):
        r = jnp.dot(
            turned[...], columns[:, 256 * t : 256 * t + 256], preferred_element_type=F32
        ).T
        r0, r1, r2, r3 = (r[64 * n : 64 * n + 64, :] for n in range(4))
        row = 192 * t
        sums[row : row + 64, :] = r3 + swap_halves(r0)
        sums[row + 64 : row + 128, :] = r0 + swap_halves(r1)
        sums[row + 128 : row + 192, :] = r1 + swap_halves(r2)
    low = low_half((16, 128))
    top_row = lax.broadcasted_iota(jnp.int32, (16, 128), 0) == 0
    bias_sum = bias_sum + swap_halves(bias_sum)
    bias_tile = jnp.where(top_row, jnp.broadcast_to(bias_sum, (16, 128)), 0.0)
    for i in range(DP):
        for m in range(TILES):
            row = 16 * (27 * i + 2 * m)
            if m < TILES - 1:
                other = swap_halves(sums[row + 16 : row + 32, :])
            else:
                other = bias_tile
            tile = jnp.where(low, sums[row : row + 16, :], other)
            packed[i, 16 * m : 16 * m + 16, :] = tile.astype(BF16)
        packed[i, PACKED:PADDED, :] = jnp.zeros((PADDED - PACKED, 128), BF16)

    rs_copies = []
    for dx, dg in RS_ORDER:
        to = lax.rem(part + dx, DP), lax.rem(spot + dg, GROUP)
        at = 8 * dx + dg
        rs_copies.append(
            pltpu.make_async_remote_copy(
                src_ref=packed.at[to[0], pl.ds(pl.multiple_of(to[1] * PIECE, PIECE), PIECE)],
                dst_ref=rs_recv.at[at],
                send_sem=rs_sems.at[0, at],
                recv_sem=rs_sems.at[1, at],
                device_id={"space": zed * GROUP + to[1], "dp": to[0]},
                device_id_type=MESH,
            )
        )
    for copy in rs_copies:
        copy.start()

    for copy in face:
        copy.wait()
    read_units(recv_gxy, recv_gz, u_xy, u_z)
    build_columns(src, nbr, u_xy, u_z, stage, columns)

    def grad_input(p):
        lanes = slice(128 * p, 128 * p + 128)
        r = lax.dot_general(
            columns[256 * p : 256 * p + 256, :],
            backward[...],
            (((1,), (1,)), ((), ())),
            preferred_element_type=F32,
        )
        grad_in[:, lanes] = (r * mask[:, lanes].astype(F32)).astype(BF16)

    for copy in rs_copies:
        copy.wait()
    mine = pl.ds(pl.multiple_of(spot * PIECE, PIECE), PIECE)
    total = packed[part, mine, :].astype(F32)
    for at in range(1, DP * GROUP):
        total += rs_recv[at].astype(F32)
    z_recv[zed] = total.astype(BF16)
    pl.semaphore_wait(ready.at[2], 2)
    z_copies = [
        pltpu.make_async_remote_copy(
            src_ref=z_recv.at[zed],
            dst_ref=z_recv.at[zed],
            send_sem=z_sems.at[0, d],
            recv_sem=z_sems.at[1, d],
            device_id=along_z(d),
            device_id_type=MESH,
        )
        for d in (8, 7, 9, 6, 10, 5, 11, 4, 12, 3, 13, 2, 14, 1, 15)
    ]
    for copy in z_copies:
        copy.start()
    for p in range(4):
        grad_input(p)

    for copy in z_copies:
        copy.wait()
    total = z_recv[0].astype(F32)
    for d in range(1, ZS):
        total += z_recv[d].astype(F32)
    full[mine, :] = total.astype(BF16)
    ag_copies = [
        pltpu.make_async_remote_copy(
            src_ref=full.at[mine],
            dst_ref=full.at[mine],
            send_sem=ag_sems.at[0, d],
            recv_sem=ag_sems.at[1, d],
            device_id=in_group(d),
            device_id_type=MESH,
        )
        for d in range(1, GROUP)
    ]
    for copy in ag_copies:
        copy.start()
    for copy in ag_copies:
        copy.wait()


def last_kernel(block_in, grad_v, full, block_out, grad_out, gw, gb, rows):
    part = lax.axis_index("dp")
    block_out[...] = block_in[...]
    grad_out[...] = grad_v[...]
    for m in range(TILES):
        tile = full[16 * m : 16 * m + 16, :].astype(F32)
        other = swap_halves(tile)
        rows[32 * m : 32 * m + 16, :] = tile
        rows[32 * m + 16 : 32 * m + 32, :] = other
        if m == TILES - 1:
            picked = jnp.zeros((16, 128), F32)
            for i in range(DP):
                turn = pltpu.roll(other, 128 - 16 * i, axis=1) if i else other
                picked = jnp.where(part == i, turn, picked)
            gb[...] = picked[0:1, 0:16]
    for n in range(4):
        tile = rows[128 * n : 128 * n + 128, :].T[0:64, :]
        if n < 3:
            gw[:, 128 * n : 128 * n + 128] = tile
        else:
            gw[:, 384:432] = tile[:, 0:48]


def vmem(n):
    return [pl.BlockSpec(memory_space=pltpu.VMEM)] * n


def smem(n):
    return [pl.BlockSpec(memory_space=pltpu.SMEM)] * n


def of(shape, dtype):
    return jax.ShapeDtypeStruct(shape, dtype)


def body(features, occupancy, counts, send_units, neighbours, weight, conv_bias, cotangent):
    shard_shape = features.shape
    sends = send_units.transpose(0, 2, 1, 3).reshape(COLS, 1, 12)
    block_out, grad_in, full = pl.pallas_call(
        main_kernel,
        out_shape=(of((ROWS, LANES), BF16), of((ROWS, LANES), BF16), of((PADDED, 128), BF16)),
        in_specs=smem(1) + [pl.BlockSpec(memory_space=pltpu.HBM)] * 7,
        out_specs=tuple(vmem(3)),
        scratch_shapes=[
            pltpu.SMEM((COLS, 1, 12), jnp.int32),
            pltpu.SMEM((4, 26), jnp.int32),
            pltpu.VMEM((ROWS, LANES), BF16),
            pltpu.VMEM((4, LANES), jnp.int32),
            pltpu.VMEM((64, 432), BF16),
            pltpu.VMEM((1, 16), BF16),
            pltpu.VMEM((ROWS, LANES), BF16),
            pltpu.VMEM((ROWS, LANES), BF16),
            pltpu.VMEM((PACKED, 128), BF16),
            pltpu.VMEM((DP, PACKED, 128), BF16),
            pltpu.VMEM((4, 40, 8, 128), F32),
            pltpu.VMEM((48, 8, LANES), F32),
            pltpu.VMEM((12, 64, 128), F32),
            pltpu.VMEM((3, 80, 1024), F32),
            pltpu.VMEM((1024, WIDE), BF16),
            pltpu.VMEM((1728, 128), F32),
            pltpu.VMEM((WIDE, 128), BF16),
            pltpu.VMEM((128, WIDE), BF16),
            pltpu.VMEM((4, ROWS, 128), F32),
            pltpu.VMEM((10, 8, LANES), F32),
        ]
        + [pltpu.VMEM((COLS, 64, LANES), BF16), pltpu.VMEM((COLS, 128, 128), BF16)] * 4
        + [
            pltpu.VMEM((128, 1024), BF16),
            pltpu.VMEM((1728, 128), F32),
            pltpu.VMEM((DP, PADDED, 128), BF16),
            pltpu.VMEM((DP * GROUP, PIECE, 128), BF16),
            pltpu.VMEM((ZS, PIECE, 128), BF16),
            pltpu.SemaphoreType.DMA((7,)),
            pltpu.SemaphoreType.DMA((2, 8)),
            pltpu.SemaphoreType.DMA((2, 8)),
            pltpu.SemaphoreType.DMA((2, DP)),
            pltpu.SemaphoreType.DMA((2, DP * GROUP)),
            pltpu.SemaphoreType.DMA((2, ZS)),
            pltpu.SemaphoreType.DMA((2, GROUP)),
            pltpu.SemaphoreType.REGULAR((3,)),
        ],
        compiler_params=pltpu.CompilerParams(
            collective_id=0, has_side_effects=True, vmem_limit_bytes=24 * 1024 * 1024
        ),
        name="main",
    )(
        counts,
        *(
            pltpu.with_memory_space_constraint(x, pltpu.HBM)
            for x in (
                features.reshape(ROWS, LANES), occupancy[0], weight.T, conv_bias.reshape(1, 16),
                cotangent.reshape(ROWS, LANES), sends, neighbours[0],
            )
        )
    )
    block_out, grad_in, gw, gb = pl.pallas_call(
        last_kernel,
        out_shape=(
            of((ROWS, LANES), BF16),
            of((ROWS, LANES), BF16),
            of((64, 432), F32),
            of((1, 16), F32),
        ),
        in_specs=vmem(3),
        out_specs=tuple(vmem(4)),
        scratch_shapes=[pltpu.VMEM((512, 128), F32)],
        compiler_params=pltpu.CompilerParams(vmem_limit_bytes=8 * 1024 * 1024),
        name="finish",
    )(block_out, grad_in, full)
    return block_out.reshape(shard_shape), grad_in.reshape(shard_shape), gw.T, gb.reshape(16)


def solution(mesh):
    placed = (
        P("dp", "space", None, None, None),
        P("dp", "space", None),
        P("dp", "space"),
        P("dp", "space", None, None),
        P("dp", "space", None),
        P("dp", None),
        P("dp"),
        P("dp", "space", None, None, None),
    )
    return jax.shard_map(
        body,
        mesh=mesh,
        in_specs=placed,
        out_specs=(
            P("dp", "space", None, None, None),
            P("dp", "space", None, None, None),
            P("dp", None),
            P("dp"),
        ),
        check_vma=False,
    )
```

```python
import jax
import jax.numpy as jnp
from jax import lax
from jax.experimental import pallas as pl
from jax.experimental.pallas import tpu as pltpu
from jax.sharding import PartitionSpec as P

F32 = jnp.float32
BF16 = jnp.bfloat16
MESH = pl.DeviceIdType.MESH
SPACE = 128
DP = 4
GROUP = 8
PAIRS = 8
COLS = 5
ROWS = 256
LANES = 512
WIDE = 2304
TILES = 14
PACKED = 224
PADDED = 256
PIECE = 16
NEAR = (1, 2, SPACE - 1, SPACE - 2)
BLOCK = [(ds, dg) for dg in (4, 5, 3, 2, 6, 7, 1, 0) for ds in (1, 0) if (ds, dg) != (0, 0)]
XY_LINKS = ((0, 1), (2, 3), (6, 7), (8, 9))


def low_half(shape):
    return lax.broadcasted_iota(jnp.int32, shape, len(shape) - 1) < 64


def near_column(step):
    return {1: 3, 2: 4, SPACE - 1: 1, SPACE - 2: 0}[step]


def swap_halves(v):
    return pltpu.roll(v, 64, axis=v.ndim - 1)


def keep(src, flat, sides, q, values):
    src[q, 0:8] = jnp.zeros((8, 8, 128), F32)
    src[q, 8:40] = values.reshape(32, 8, 128)
    flat[q] = values
    for y in range(2):
        sides[5 * y, :, 128 * q : 128 * q + 128] = jnp.zeros((8, 128), F32)
        for b in range(4):
            rows = pl.ds(64 * b + 7 * y, 8, stride=8)
            sides[5 * y + b + 1, :, 128 * q : 128 * q + 128] = flat[q, rows, :]


def pack_faces(src, sides, snd, out_xy, out_z):
    def slot_of(column, link):
        return ((snd[column, 0, link] + 6) * 43) >> 8

    def plane(column, link):
        slot = slot_of(column, link)
        face = link % 6
        if face >= 2:
            return sides[5 * (face - 2) + slot]
        return jnp.concatenate([src[q, slot * 8 + 7 * face] for q in range(4)], axis=1)

    low = low_half((64, 128))
    for column in range(COLS):
        for q, pair in enumerate(XY_LINKS):
            both = jnp.concatenate([plane(column, link) for link in pair], axis=0)
            out_xy[column, 16 * q : 16 * q + 16, :] = both.astype(BF16)
        for h in range(2):
            first = src[0, pl.ds(slot_of(column, 4 + 6 * h) * 8, 8)].reshape(64, 128)
            last = src[3, pl.ds(slot_of(column, 5 + 6 * h) * 8, 8)].reshape(64, 128)
            both = jnp.where(low, first, last)
            out_z[column, 64 * h : 64 * h + 64, :] = both.astype(BF16)


def face_copies(send_xy, send_z, recv_xy, recv_z, sems):
    me = lax.axis_index("space")
    copies = []
    for step in NEAR:
        column = near_column(step)
        for m, (src, dst) in enumerate(((send_xy, recv_xy), (send_z, recv_z))):
            copies.append(
                pltpu.make_async_remote_copy(
                    src_ref=src.at[column],
                    dst_ref=dst.at[column],
                    send_sem=sems.at[0, m],
                    recv_sem=sems.at[1, m],
                    device_id={"space": lax.rem(me + step, SPACE)},
                    device_id_type=MESH,
                )
            )
    return copies


def wait_bytes(view, send_sem, recv_sem):
    peer = lax.rem(lax.axis_index("space") + 1, SPACE)
    pltpu.make_async_remote_copy(
        src_ref=view,
        dst_ref=view,
        send_sem=send_sem,
        recv_sem=recv_sem,
        device_id={"space": peer},
        device_id_type=MESH,
    ).wait()


def wait_faces(recv_xy, recv_z, sems):
    wait_bytes(recv_xy.at[pl.ds(0, 4)], sems.at[0, 0], sems.at[1, 0])
    wait_bytes(recv_z.at[pl.ds(0, 4)], sems.at[0, 1], sems.at[1, 1])


def own_faces(send_xy, send_z, recv_xy, recv_z):
    recv_xy[2] = send_xy[2]
    recv_z[2] = send_z[2]


def pack_weights(wt, bias, wsend):
    row = jnp.concatenate([bias[...].astype(F32), jnp.zeros((1, 48), F32)], axis=1)
    first = lax.broadcasted_iota(jnp.int32, (16, 64), 0) == 0
    last = jnp.where(first, jnp.broadcast_to(row, (16, 64)), 0.0)
    for n in range(4):
        if n < 3:
            tile = wt[:, 128 * n : 128 * n + 128].astype(F32)
        else:
            tile = jnp.concatenate([wt[:, 384:432].astype(F32), jnp.zeros((64, 80), F32)], axis=1)
        tile = tile.T
        for m in range(4 if n < 3 else 2):
            other = tile[32 * m + 16 : 32 * m + 32] if 4 * n + m < TILES - 1 else last
            both = jnp.concatenate([tile[32 * m : 32 * m + 16], other], axis=1)
            wsend[64 * n + 16 * m : 64 * n + 16 * m + 16, :] = both.astype(BF16)


def mask_parts():
    place = lax.broadcasted_iota(jnp.int32, (64, LANES), 1)
    owner = (place >> 3) == lax.broadcasted_iota(jnp.int32, (64, LANES), 0)
    fold = lax.broadcasted_iota(jnp.int32, (LANES, 128), 0) & 7
    fold = (fold == lax.broadcasted_iota(jnp.int32, (LANES, 128), 1)).astype(F32).astype(BF16)
    widen = lax.broadcasted_iota(jnp.int32, (128, LANES), 1) >> 6
    widen = (widen == lax.broadcasted_iota(jnp.int32, (128, LANES), 0)).astype(F32).astype(BF16)
    return owner.astype(F32), fold, widen


def expand_mask(occ, cnt, owner, fold, widen):
    spread = []
    for b in range(4):
        live = jnp.minimum(jnp.maximum(cnt[0, 0] - b, 0), 1)
        row = (occ[b : b + 1, :] * live).astype(F32)
        spread.append(owner * jnp.broadcast_to(row, (64, LANES)))
    by_z = jnp.dot(jnp.concatenate(spread, axis=0).astype(BF16), fold, preferred_element_type=F32)
    return jnp.dot(by_z.astype(BF16), widen, preferred_element_type=F32)


def read_units(units_xy, units_z, u_xy, u_z):
    for column in range(COLS):
        planes = units_xy[column].astype(F32)
        u_xy[8 * column + 8 : 8 * column + 16] = planes.reshape(8, 8, LANES)
        planes = units_z[column].astype(F32)
        u_z[2 * column + 2 : 2 * column + 4] = planes.reshape(2, 64, 128)


def build_columns(src, nbr, u_xy, u_z, stage, columns):
    low = low_half((8, 128))
    low_row = low_half((1, 128))
    depth = lax.broadcasted_iota(jnp.int32, (8, 640), 0)

    def one_brick(b, carry):
        where_of = {}
        for first in range(3):
            for second in range(3):
                for third in range(3):
                    o = (first - 1, second - 1, third - 1)
                    k = first * 9 + second * 3 + third
                    if k == 13:
                        continue
                    n = nbr[b, k if k < 13 else k - 1] + 12
                    column = (n * 171) >> 11
                    upper = (n - column * 12 + 2) >> 3
                    d = 0 if o[0] else 1 if o[1] else 2
                    face = 2 * d + (0 if o[d] == 1 else 1)
                    if d < 2:
                        where_of[o] = column * 8 + face + 4 * upper
                    else:
                        where_of[o] = column * 2 + upper

        def expand(c):
            t = [c[:, 128 * i : 128 * i + 128] for i in range(5)]
            return jnp.concatenate(
                [
                    t[0], jnp.where(low, t[1], t[4]),
                    t[1], jnp.where(low, t[2], t[0]),
                    t[2], jnp.where(low, t[3], t[1]),
                    t[3], jnp.where(low, t[4], t[2]),
                ],
                axis=1,
            )

        def side_row(ox, oy, row):
            rows = slice(row, row + 1)
            middle = u_xy[where_of[ox, oy, 0], rows, :]
            after = u_xy[where_of[ox, oy, 1], rows, 0:128]
            before = u_xy[where_of[ox, oy, -1], rows, 384:512]
            return jnp.concatenate([middle, jnp.where(low_row, after, before)], axis=1)

        for xx in range(10):
            if 1 <= xx <= 8:
                here = jnp.concatenate([src[q, b * 8 + 7 + xx] for q in range(4)], axis=1)
                rows = slice(8 * xx - 8, 8 * xx)
                after = u_z[where_of[0, 0, 1], rows, :]
                before = u_z[where_of[0, 0, -1], rows, :]
                lower, upper = side_row(0, -1, xx - 1), side_row(0, 1, xx - 1)
            else:
                ox = -1 if xx == 0 else 1
                here = u_xy[where_of[ox, 0, 0]]
                after = u_xy[where_of[ox, 0, 1], :, 0:128]
                before = u_xy[where_of[ox, 0, -1], :, 384:512]
                lower, upper = side_row(ox, -1, 7), side_row(ox, 1, 0)
            c = jnp.concatenate([here, jnp.where(low, after, before)], axis=1)
            down = jnp.where(depth == 0, jnp.broadcast_to(lower, (8, 640)), pltpu.roll(c, 1, axis=0))
            up = jnp.where(depth == 7, jnp.broadcast_to(upper, (8, 640)), pltpu.roll(c, 7, axis=0))
            for e, tile in enumerate((down, c, up)):
                stage[e, 8 * xx : 8 * xx + 8, :] = expand(tile)
        for a in range(3):
            for e in range(3):
                t = 3 * a + e
                for p in range(4):
                    rows = pl.ds(pl.multiple_of(b * 64, 64) + 256 * p, 64)
                    columns[rows, 256 * t : 256 * t + 256] = stage[
                        e, 8 * a : 8 * a + 64, 256 * p : 256 * p + 256
                    ].astype(BF16)
        return carry

    lax.fori_loop(0, 4, one_brick, 0)


def build_bands(wall, both, forward, backward):
    low = low_half((16, 128))
    for i in range(DP):
        for m in range(TILES):
            tile = wall[i, 16 * m : 16 * m + 16, :].astype(F32)
            turned = swap_halves(tile)
            row = 16 * (27 * i + 2 * m)
            both[row : row + 16, :] = jnp.where(low, tile, turned)
            if m < TILES - 1:
                both[row + 16 : row + 32, :] = jnp.where(low, turned, tile)
    low = low_half((64, 128))
    for t in range(9):
        w0, w1, w2 = (both[64 * (3 * t + f) : 64 * (3 * t + f) + 64, :] for f in range(3))
        parts = [
            jnp.where(low, w1, w0),
            jnp.where(low, w2, w1),
            jnp.where(low, 0.0, w2),
            jnp.where(low, w0, 0.0),
        ]
        for n, part in enumerate(parts):
            part = part.astype(BF16)
            row = 256 * t + 64 * n
            forward[row : row + 64, :] = part
            lane = 256 * (8 - t) + 128 * (n // 2)
            row = 64 * (n % 2)
            backward[row : row + 64, lane : lane + 128] = part


def whole_bias(wall):
    lane = lax.broadcasted_iota(jnp.int32, (16, 128), 1)
    total = jnp.zeros((16, 128), F32)
    for i in range(DP):
        tile = wall[i, PACKED - 16 : PACKED, :].astype(F32)
        tile = jnp.where((lane >= 64) & (lane < 80), tile, 0.0)
        total += pltpu.roll(tile, 64 + 16 * i, axis=1)
        total += pltpu.roll(tile, 16 * i, axis=1) if i else tile
    return total[0:1, :]


def main_kernel(
    cnt, feat, occ, wt, bias, cot, snd_in, nbr_in,
    block_out, grad_in, full,
    snd, nbr, feat_v, occ_v, wt_v, bias_v, cot_v, mask, wsend, wall,
    src, u_xy, u_z, stage, columns, both, forward, backward,
    flat, sides, send_xy, send_z, recv_xy, recv_z, send_gxy, send_gz, recv_gxy, recv_gz, turned,
    sums, packed, rs_recv, z_recv,
    in_sems, sems, gsems, wsems, rs_sems, z_sems, ag_sems, ready,
):
    me, part = lax.axis_index("space"), lax.axis_index("dp")
    zed, spot = me // GROUP, lax.rem(me, GROUP)
    pair, side = zed // 2, lax.rem(zed, 2)
    barrier = pltpu.get_barrier_semaphore()

    def in_group(d):
        return {"space": zed * GROUP + lax.rem(spot + d, GROUP)}

    def along_z(d):
        return {"space": lax.rem(zed + d, 2 * PAIRS) * GROUP + spot}

    def in_block(ds, dg):
        to = lax.rem(side + ds, 2), lax.rem(spot + dg, GROUP)
        return (2 * pair + to[0]) * GROUP + to[1], to[0] * GROUP + to[1]

    def along_dp(d):
        return {"dp": lax.rem(part + d, DP)}

    def tell(sem, peers):
        for peer in peers:
            pl.semaphore_signal(sem, inc=1, device_id=peer, device_id_type=MESH)

    across = [along_dp(d) for d in range(1, DP)]
    beside = [along_z(1), along_z(2 * PAIRS - 1)]
    near = [{"space": lax.rem(me + step, SPACE)} for step in NEAR]
    around = [in_group(d) for d in range(1, GROUP)]
    near += across + beside + around
    loads = [
        pltpu.make_async_copy(far, here, in_sems.at[n])
        for n, (far, here) in enumerate(
            (
                (occ, occ_v), (feat, feat_v), (wt, wt_v), (bias, bias_v), (cot, cot_v),
                (snd_in, snd), (nbr_in, nbr),
            )
        )
    ]
    for load in loads:
        load.start()
    tell(barrier, near)

    constants = mask_parts()
    for n in (2, 3):
        loads[n].wait()
    pack_weights(wt_v, bias_v, wsend)
    loads[0].wait()
    active = expand_mask(occ_v, cnt, *constants)
    mask[...] = active.astype(BF16)
    loads[1].wait()
    values = feat_v[...].astype(F32) * active
    for q in range(4):
        keep(src, flat, sides, q, values[:, 128 * q : 128 * q + 128])
    loads[5].wait()
    pack_faces(src, sides, snd, send_xy, send_z)

    pl.semaphore_wait(barrier, len(near))
    copies = face_copies(send_xy, send_z, recv_xy, recv_z, sems)
    shares = [
        pltpu.make_async_remote_copy(
            src_ref=wsend,
            dst_ref=wall.at[part],
            send_sem=wsems.at[0],
            recv_sem=wsems.at[1],
            device_id=along_dp(d),
            device_id_type=MESH,
        )
        for d in range(1, DP)
    ]
    for copy in copies + shares:
        copy.start()
    tell(ready.at[0], across + beside + around)
    wall[part] = wsend[...]
    own_faces(send_xy, send_z, recv_xy, recv_z)
    u_xy[0:8] = jnp.zeros((8, 8, LANES), F32)
    u_z[0:2] = jnp.zeros((2, 64, 128), F32)
    wait_bytes(wall.at[pl.ds(0, DP - 1)], wsems.at[0], wsems.at[1])
    build_bands(wall, both, forward, backward)
    bias_row = whole_bias(wall)
    wait_faces(recv_xy, recv_z, sems)
    pl.semaphore_wait(ready.at[0], len(across) + len(beside) + len(around))
    tell(ready.at[1], across + [along_z(2), along_z(2 * PAIRS - 2)])

    loads[6].wait()
    read_units(recv_xy, recv_z, u_xy, u_z)
    build_columns(src, nbr, u_xy, u_z, stage, columns)
    loads[4].wait()
    bias_sum = jnp.zeros((1, 128), F32)
    for p in range(4):
        lanes = slice(128 * p, 128 * p + 128)
        pre = jnp.dot(
            columns[256 * p : 256 * p + 256, :], forward[...], preferred_element_type=F32
        )
        pre = pre + bias_row
        sig = jax.nn.sigmoid(pre)
        on = mask[:, lanes].astype(F32)
        block_out[:, lanes] = (pre * sig * on).astype(BF16)
        g = cot_v[:, lanes].astype(F32) * sig * (1.0 + pre * (1.0 - sig)) * on
        g = g.astype(BF16).astype(F32)
        keep(src, flat, sides, p, g)
        turned[:, 256 * p : 256 * p + 256] = g.T.astype(BF16)
        bias_sum += jnp.sum(g, axis=0, keepdims=True)
    pl.semaphore_wait(ready.at[1], len(across) + 2)
    tell(ready.at[2], [along_z(4), along_z(2 * PAIRS - 4)])

    low = low_half((16, 128))
    top_row = lax.broadcasted_iota(jnp.int32, (16, 128), 0) == 0
    bias_sum = bias_sum + swap_halves(bias_sum)
    bias_tile = jnp.where(top_row, jnp.broadcast_to(bias_sum, (16, 128)), 0.0)

    def reduce_copy(i, ds, dg):
        to, place = in_block(ds, dg)
        at = 2 * GROUP * lax.rem(i - part + DP, DP) + GROUP * ds + dg
        return pltpu.make_async_remote_copy(
            src_ref=packed.at[i, pl.ds(pl.multiple_of(place * PIECE, PIECE), PIECE)],
            dst_ref=rs_recv.at[at],
            send_sem=rs_sems.at[0],
            recv_sem=rs_sems.at[1],
            device_id={"space": to, "dp": i},
            device_id_type=MESH,
        )

    done = 0
    for owners, upto in (((0,), 3), ((1,), 5), ((2,), 7), ((3,), 9)):
        for t in range(done, upto):
            r = jnp.dot(
                turned[...], columns[:, 256 * t : 256 * t + 256], preferred_element_type=F32
            ).T
            r0, r1, r2, r3 = (r[64 * n : 64 * n + 64, :] for n in range(4))
            row = 192 * t
            sums[row : row + 64, :] = r3 + swap_halves(r0)
            sums[row + 64 : row + 128, :] = r0 + swap_halves(r1)
            sums[row + 128 : row + 192, :] = r1 + swap_halves(r2)
        done = upto
        for i in owners:
            for m in range(TILES):
                row = 16 * (27 * i + 2 * m)
                if m < TILES - 1:
                    other = swap_halves(sums[row + 16 : row + 32, :])
                else:
                    other = bias_tile
                tile = jnp.where(low, sums[row : row + 16, :], other)
                packed[i, 16 * m : 16 * m + 16, :] = tile.astype(BF16)
            packed[i, PACKED:PADDED, :] = jnp.zeros((PADDED - PACKED, 128), BF16)
        for i in owners:
            for ds, dg in BLOCK:
                reduce_copy(i, ds, dg).start()
        for i in owners:

            @pl.when(part != i)
            def _(i=i):
                reduce_copy(i, 0, 0).start()

    pack_faces(src, sides, snd, send_gxy, send_gz)
    face = face_copies(send_gxy, send_gz, recv_gxy, recv_gz, gsems)
    for copy in face:
        copy.start()
    own_faces(send_gxy, send_gz, recv_gxy, recv_gz)

    def grad_input(p):
        lanes = slice(128 * p, 128 * p + 128)
        r = lax.dot_general(
            columns[256 * p : 256 * p + 256, :],
            backward[...],
            (((1,), (1,)), ((), ())),
            preferred_element_type=F32,
        )
        grad_in[:, lanes] = (r * mask[:, lanes].astype(F32)).astype(BF16)

    wait_bytes(rs_recv.at[pl.ds(1, 2 * DP * GROUP - 1)], rs_sems.at[0], rs_sems.at[1])
    mine = pl.ds(pl.multiple_of((side * GROUP + spot) * PIECE, PIECE), PIECE)
    total = packed[part, mine, :].astype(F32)
    for at in range(1, 2 * DP * GROUP):
        total += rs_recv[at].astype(F32)
    z_recv[pair] = total.astype(BF16)
    pl.semaphore_wait(ready.at[2], 2)
    for d in (4, 3, 5, 2, 6, 1, 7):
        pltpu.make_async_remote_copy(
            src_ref=z_recv.at[pair],
            dst_ref=z_recv.at[pair],
            send_sem=z_sems.at[0],
            recv_sem=z_sems.at[1],
            device_id={"space": (2 * lax.rem(pair + d, PAIRS) + side) * GROUP + spot},
            device_id_type=MESH,
        ).start()
    wait_faces(recv_gxy, recv_gz, gsems)
    read_units(recv_gxy, recv_gz, u_xy, u_z)
    build_columns(src, nbr, u_xy, u_z, stage, columns)
    for p in range(4):
        grad_input(p)

    wait_bytes(z_recv.at[pl.ds(0, PAIRS - 1)], z_sems.at[0], z_sems.at[1])
    total = z_recv[0].astype(F32)
    for d in range(1, PAIRS):
        total += z_recv[d].astype(F32)
    full[mine, :] = total.astype(BF16)
    for ds, dg in BLOCK:
        pltpu.make_async_remote_copy(
            src_ref=full.at[mine],
            dst_ref=full.at[mine],
            send_sem=ag_sems.at[0],
            recv_sem=ag_sems.at[1],
            device_id={"space": in_block(ds, dg)[0]},
            device_id_type=MESH,
        ).start()
    wait_bytes(full.at[pl.ds(0, (2 * GROUP - 1) * PIECE)], ag_sems.at[0], ag_sems.at[1])


def last_kernel(block_in, grad_v, full, block_out, grad_out, gw, gb, rows):
    part = lax.axis_index("dp")
    block_out[...] = block_in[...]
    grad_out[...] = grad_v[...]
    for m in range(TILES):
        tile = full[16 * m : 16 * m + 16, :].astype(F32)
        other = swap_halves(tile)
        rows[32 * m : 32 * m + 16, :] = tile
        rows[32 * m + 16 : 32 * m + 32, :] = other
        if m == TILES - 1:
            picked = jnp.zeros((16, 128), F32)
            for i in range(DP):
                turn = pltpu.roll(other, 128 - 16 * i, axis=1) if i else other
                picked = jnp.where(part == i, turn, picked)
            gb[...] = picked[0:1, 0:16]
    for n in range(4):
        tile = rows[128 * n : 128 * n + 128, :].T[0:64, :]
        if n < 3:
            gw[:, 128 * n : 128 * n + 128] = tile
        else:
            gw[:, 384:432] = tile[:, 0:48]


def vmem(n):
    return [pl.BlockSpec(memory_space=pltpu.VMEM)] * n


def smem(n):
    return [pl.BlockSpec(memory_space=pltpu.SMEM)] * n


def of(shape, dtype):
    return jax.ShapeDtypeStruct(shape, dtype)


def body(features, occupancy, counts, send_units, neighbours, weight, conv_bias, cotangent):
    shard_shape = features.shape
    sends = send_units.transpose(0, 2, 1, 3).reshape(COLS, 1, 12)
    block_out, grad_in, full = pl.pallas_call(
        main_kernel,
        out_shape=(of((ROWS, LANES), BF16), of((ROWS, LANES), BF16), of((PADDED, 128), BF16)),
        in_specs=smem(1) + [pl.BlockSpec(memory_space=pltpu.HBM)] * 7,
        out_specs=tuple(vmem(3)),
        scratch_shapes=[
            pltpu.SMEM((COLS, 1, 12), jnp.int32),
            pltpu.SMEM((4, 26), jnp.int32),
            pltpu.VMEM((ROWS, LANES), BF16),
            pltpu.VMEM((4, LANES), jnp.int32),
            pltpu.VMEM((64, 432), BF16),
            pltpu.VMEM((1, 16), BF16),
            pltpu.VMEM((ROWS, LANES), BF16),
            pltpu.VMEM((ROWS, LANES), BF16),
            pltpu.VMEM((PACKED, 128), BF16),
            pltpu.VMEM((DP, PACKED, 128), BF16),
            pltpu.VMEM((4, 40, 8, 128), F32),
            pltpu.VMEM((48, 8, LANES), F32),
            pltpu.VMEM((12, 64, 128), F32),
            pltpu.VMEM((3, 80, 1024), F32),
            pltpu.VMEM((1024, WIDE), BF16),
            pltpu.VMEM((1728, 128), F32),
            pltpu.VMEM((WIDE, 128), BF16),
            pltpu.VMEM((128, WIDE), BF16),
            pltpu.VMEM((4, ROWS, 128), F32),
            pltpu.VMEM((10, 8, LANES), F32),
        ]
        + [pltpu.VMEM((COLS, 64, LANES), BF16), pltpu.VMEM((COLS, 128, 128), BF16)] * 4
        + [
            pltpu.VMEM((128, 1024), BF16),
            pltpu.VMEM((1728, 128), F32),
            pltpu.VMEM((DP, PADDED, 128), BF16),
            pltpu.VMEM((2 * DP * GROUP, PIECE, 128), BF16),
            pltpu.VMEM((PAIRS, PIECE, 128), BF16),
            pltpu.SemaphoreType.DMA((7,)),
            pltpu.SemaphoreType.DMA((2, 2)),
            pltpu.SemaphoreType.DMA((2, 2)),
            pltpu.SemaphoreType.DMA((2,)),
            pltpu.SemaphoreType.DMA((2,)),
            pltpu.SemaphoreType.DMA((2,)),
            pltpu.SemaphoreType.DMA((2,)),
            pltpu.SemaphoreType.REGULAR((3,)),
        ],
        compiler_params=pltpu.CompilerParams(
            collective_id=0, has_side_effects=True, vmem_limit_bytes=24 * 1024 * 1024
        ),
        name="main",
    )(
        counts,
        *(
            pltpu.with_memory_space_constraint(x, pltpu.HBM)
            for x in (
                features.reshape(ROWS, LANES), occupancy[0], weight.T, conv_bias.reshape(1, 16),
                cotangent.reshape(ROWS, LANES), sends, neighbours[0],
            )
        )
    )
    block_out, grad_in, gw, gb = pl.pallas_call(
        last_kernel,
        out_shape=(
            of((ROWS, LANES), BF16),
            of((ROWS, LANES), BF16),
            of((64, 432), F32),
            of((1, 16), F32),
        ),
        in_specs=vmem(3),
        out_specs=tuple(vmem(4)),
        scratch_shapes=[pltpu.VMEM((512, 128), F32)],
        compiler_params=pltpu.CompilerParams(vmem_limit_bytes=8 * 1024 * 1024),
        name="finish",
    )(block_out, grad_in, full)
    return block_out.reshape(shard_shape), grad_in.reshape(shard_shape), gw.T, gb.reshape(16)


def solution(mesh):
    placed = (
        P("dp", "space", None, None, None),
        P("dp", "space", None),
        P("dp", "space"),
        P("dp", "space", None, None),
        P("dp", "space", None),
        P("dp", None),
        P("dp"),
        P("dp", "space", None, None, None),
    )
    return jax.shard_map(
        body,
        mesh=mesh,
        in_specs=placed,
        out_specs=(
            P("dp", "space", None, None, None),
            P("dp", "space", None, None, None),
            P("dp", None),
            P("dp"),
        ),
        check_vma=False,
    )
```

```python
import jax
import jax.numpy as jnp
from jax import lax
from jax.experimental import pallas as pl
from jax.experimental.pallas import tpu as pltpu
from jax.sharding import PartitionSpec as P

F32 = jnp.float32
BF16 = jnp.bfloat16
MESH = pl.DeviceIdType.MESH
SPACE = 128
DP = 4
GROUP = 8
PAIRS = 8
COLS = 5
ROWS = 256
LANES = 512
WIDE = 2304
TILES = 14
PACKED = 224
PADDED = 256
PIECE = 16
NEAR = (1, 2, SPACE - 1, SPACE - 2)
BLOCK = [(ds, dg) for dg in (4, 5, 3, 2, 6, 7, 1, 0) for ds in (1, 0) if (ds, dg) != (0, 0)]
XY_LINKS = ((0, 1), (2, 3), (6, 7), (8, 9))


def low_half(shape):
    return lax.broadcasted_iota(jnp.int32, shape, len(shape) - 1) < 64


def near_column(step):
    return {1: 3, 2: 4, SPACE - 1: 1, SPACE - 2: 0}[step]


def swap_halves(v):
    return pltpu.roll(v, 64, axis=v.ndim - 1)


def keep(src, flat, sides, q, values):
    src[q, 0:8] = jnp.zeros((8, 8, 128), F32)
    src[q, 8:40] = values.reshape(32, 8, 128)
    flat[q] = values
    for y in range(2):
        sides[5 * y, :, 128 * q : 128 * q + 128] = jnp.zeros((8, 128), F32)
        for b in range(4):
            rows = pl.ds(64 * b + 7 * y, 8, stride=8)
            sides[5 * y + b + 1, :, 128 * q : 128 * q + 128] = flat[q, rows, :]


def pack_faces(src, sides, snd, out_xy, out_z):
    def slot_of(column, link):
        return ((snd[column, 0, link] + 6) * 43) >> 8

    def plane(column, link):
        slot = slot_of(column, link)
        face = link % 6
        if face >= 2:
            return sides[5 * (face - 2) + slot]
        return jnp.concatenate([src[q, slot * 8 + 7 * face] for q in range(4)], axis=1)

    low = low_half((64, 128))
    for column in range(COLS):
        for q, pair in enumerate(XY_LINKS):
            both = jnp.concatenate([plane(column, link) for link in pair], axis=0)
            out_xy[column, 16 * q : 16 * q + 16, :] = both.astype(BF16)
        for h in range(2):
            first = src[0, pl.ds(slot_of(column, 4 + 6 * h) * 8, 8)].reshape(64, 128)
            last = src[3, pl.ds(slot_of(column, 5 + 6 * h) * 8, 8)].reshape(64, 128)
            both = jnp.where(low, first, last)
            out_z[column, 64 * h : 64 * h + 64, :] = both.astype(BF16)


def face_copies(send_xy, send_z, recv_xy, recv_z, sems):
    me = lax.axis_index("space")
    copies = []
    for step in NEAR:
        column = near_column(step)
        for m, (src, dst) in enumerate(((send_xy, recv_xy), (send_z, recv_z))):
            copies.append(
                pltpu.make_async_remote_copy(
                    src_ref=src.at[column],
                    dst_ref=dst.at[column],
                    send_sem=sems.at[0, m],
                    recv_sem=sems.at[1, m],
                    device_id={"space": lax.rem(me + step, SPACE)},
                    device_id_type=MESH,
                )
            )
    return copies


def copies_of(view, send_sem, recv_sem):
    peer = lax.rem(lax.axis_index("space") + 1, SPACE)
    return pltpu.make_async_remote_copy(
        src_ref=view,
        dst_ref=view,
        send_sem=send_sem,
        recv_sem=recv_sem,
        device_id={"space": peer},
        device_id_type=MESH,
    )


def wait_bytes(view, send_sem, recv_sem):
    copies_of(view, send_sem, recv_sem).wait()


def wait_faces(recv_xy, recv_z, sems):
    wait_bytes(recv_xy.at[pl.ds(0, 4)], sems.at[0, 0], sems.at[1, 0])
    wait_bytes(recv_z.at[pl.ds(0, 4)], sems.at[0, 1], sems.at[1, 1])


def own_faces(send_xy, send_z, recv_xy, recv_z):
    recv_xy[2] = send_xy[2]
    recv_z[2] = send_z[2]


def pack_weights(wt, bias, wsend):
    row = jnp.concatenate([bias[...].astype(F32), jnp.zeros((1, 48), F32)], axis=1)
    first = lax.broadcasted_iota(jnp.int32, (16, 64), 0) == 0
    last = jnp.where(first, jnp.broadcast_to(row, (16, 64)), 0.0)
    for n in range(4):
        if n < 3:
            tile = wt[:, 128 * n : 128 * n + 128].astype(F32)
        else:
            tile = jnp.concatenate([wt[:, 384:432].astype(F32), jnp.zeros((64, 80), F32)], axis=1)
        tile = tile.T
        for m in range(4 if n < 3 else 2):
            other = tile[32 * m + 16 : 32 * m + 32] if 4 * n + m < TILES - 1 else last
            both = jnp.concatenate([tile[32 * m : 32 * m + 16], other], axis=1)
            wsend[64 * n + 16 * m : 64 * n + 16 * m + 16, :] = both.astype(BF16)


def mask_parts():
    place = lax.broadcasted_iota(jnp.int32, (64, LANES), 1)
    owner = (place >> 3) == lax.broadcasted_iota(jnp.int32, (64, LANES), 0)
    fold = lax.broadcasted_iota(jnp.int32, (LANES, 128), 0) & 7
    fold = (fold == lax.broadcasted_iota(jnp.int32, (LANES, 128), 1)).astype(F32).astype(BF16)
    widen = lax.broadcasted_iota(jnp.int32, (128, LANES), 1) >> 6
    widen = (widen == lax.broadcasted_iota(jnp.int32, (128, LANES), 0)).astype(F32).astype(BF16)
    return owner.astype(F32), fold, widen


def expand_mask(occ, cnt, owner, fold, widen):
    spread = []
    for b in range(4):
        live = jnp.minimum(jnp.maximum(cnt[0, 0] - b, 0), 1)
        row = (occ[b : b + 1, :] * live).astype(F32)
        spread.append(owner * jnp.broadcast_to(row, (64, LANES)))
    by_z = jnp.dot(jnp.concatenate(spread, axis=0).astype(BF16), fold, preferred_element_type=F32)
    return jnp.dot(by_z.astype(BF16), widen, preferred_element_type=F32)


def read_units(units_xy, units_z, u_xy, u_z):
    for column in range(COLS):
        planes = units_xy[column].astype(F32)
        u_xy[8 * column + 8 : 8 * column + 16] = planes.reshape(8, 8, LANES)
        planes = units_z[column].astype(F32)
        u_z[2 * column + 2 : 2 * column + 4] = planes.reshape(2, 64, 128)


def build_columns(src, nbr, u_xy, u_z, columns):
    low = low_half((8, 128))
    low_row = low_half((1, 128))
    depth = lax.broadcasted_iota(jnp.int32, (8, 640), 0)

    def one_brick(b, carry):
        where_of = {}
        for first in range(3):
            for second in range(3):
                for third in range(3):
                    o = (first - 1, second - 1, third - 1)
                    k = first * 9 + second * 3 + third
                    if k == 13:
                        continue
                    n = nbr[b, k if k < 13 else k - 1] + 12
                    column = (n * 171) >> 11
                    upper = (n - column * 12 + 2) >> 3
                    d = 0 if o[0] else 1 if o[1] else 2
                    face = 2 * d + (0 if o[d] == 1 else 1)
                    if d < 2:
                        where_of[o] = column * 8 + face + 4 * upper
                    else:
                        where_of[o] = column * 2 + upper

        def expand(c):
            t = [c[:, 128 * i : 128 * i + 128] for i in range(5)]
            return jnp.concatenate(
                [
                    t[0], jnp.where(low, t[1], t[4]),
                    t[1], jnp.where(low, t[2], t[0]),
                    t[2], jnp.where(low, t[3], t[1]),
                    t[3], jnp.where(low, t[4], t[2]),
                ],
                axis=1,
            )

        def side_row(ox, oy, row):
            rows = slice(row, row + 1)
            middle = u_xy[where_of[ox, oy, 0], rows, :]
            after = u_xy[where_of[ox, oy, 1], rows, 0:128]
            before = u_xy[where_of[ox, oy, -1], rows, 384:512]
            return jnp.concatenate([middle, jnp.where(low_row, after, before)], axis=1)

        for xx in range(10):
            if 1 <= xx <= 8:
                here = jnp.concatenate([src[q, b * 8 + 7 + xx] for q in range(4)], axis=1)
                rows = slice(8 * xx - 8, 8 * xx)
                after = u_z[where_of[0, 0, 1], rows, :]
                before = u_z[where_of[0, 0, -1], rows, :]
                lower, upper = side_row(0, -1, xx - 1), side_row(0, 1, xx - 1)
            else:
                ox = -1 if xx == 0 else 1
                here = u_xy[where_of[ox, 0, 0]]
                after = u_xy[where_of[ox, 0, 1], :, 0:128]
                before = u_xy[where_of[ox, 0, -1], :, 384:512]
                lower, upper = side_row(ox, -1, 7), side_row(ox, 1, 0)
            c = jnp.concatenate([here, jnp.where(low, after, before)], axis=1)
            down = jnp.where(depth == 0, jnp.broadcast_to(lower, (8, 640)), pltpu.roll(c, 1, axis=0))
            up = jnp.where(depth == 7, jnp.broadcast_to(upper, (8, 640)), pltpu.roll(c, 7, axis=0))
            tiles = [expand(tile) for tile in (down, c, up)]
            for e in range(3) if xx else ():
                pair = jnp.concatenate([before_tiles[e], tiles[e]], axis=0).astype(BF16)
                for a in range(3):
                    x = xx - 1 - a
                    if x not in (0, 2, 4, 6):
                        continue
                    lane = 256 * (3 * a + e)
                    for p in range(4):
                        rows = pl.ds(pl.multiple_of(b * 64, 64) + 256 * p + 8 * x, 16)
                        columns[rows, lane : lane + 256] = pair[:, 256 * p : 256 * p + 256]
            before_tiles = tiles
        return carry

    lax.fori_loop(0, 4, one_brick, 0, unroll=True)


def build_bands(wall, both, forward, backward):
    low = low_half((16, 128))
    for i in range(DP):
        for m in range(TILES):
            tile = wall[i, 16 * m : 16 * m + 16, :].astype(F32)
            turned = swap_halves(tile)
            row = 16 * (27 * i + 2 * m)
            both[row : row + 16, :] = jnp.where(low, tile, turned)
            if m < TILES - 1:
                both[row + 16 : row + 32, :] = jnp.where(low, turned, tile)
    low = low_half((64, 128))
    for t in range(9):
        w0, w1, w2 = (both[64 * (3 * t + f) : 64 * (3 * t + f) + 64, :] for f in range(3))
        parts = [
            jnp.where(low, w1, w0),
            jnp.where(low, w2, w1),
            jnp.where(low, 0.0, w2),
            jnp.where(low, w0, 0.0),
        ]
        for n, part in enumerate(parts):
            part = part.astype(BF16)
            row = 256 * t + 64 * n
            forward[row : row + 64, :] = part
            lane = 256 * (8 - t) + 128 * (n // 2)
            row = 64 * (n % 2)
            backward[row : row + 64, lane : lane + 128] = part


def whole_bias(wall):
    lane = lax.broadcasted_iota(jnp.int32, (16, 128), 1)
    total = jnp.zeros((16, 128), F32)
    for i in range(DP):
        tile = wall[i, PACKED - 16 : PACKED, :].astype(F32)
        tile = jnp.where((lane >= 64) & (lane < 80), tile, 0.0)
        total += pltpu.roll(tile, 64 + 16 * i, axis=1)
        total += pltpu.roll(tile, 16 * i, axis=1) if i else tile
    return total[0:1, :]


def main_kernel(
    cnt, feat, occ, wt, bias, cot, snd_in, nbr_in,
    block_out, grad_in, full,
    snd, nbr, feat_v, occ_v, wt_v, bias_v, cot_v, mask, wsend, wall,
    src, u_xy, u_z, columns, both, forward, backward,
    flat, sides, send_xy, send_z, recv_xy, recv_z, send_gxy, send_gz, recv_gxy, recv_gz, turned,
    sums, packed, rs_recv, z_recv,
    in_sems, sems, gsems, wsems, rs_sems, z_sems, ag_sems, ready,
):
    me, part = lax.axis_index("space"), lax.axis_index("dp")
    zed, spot = me // GROUP, lax.rem(me, GROUP)
    pair, side = zed // 2, lax.rem(zed, 2)
    barrier = pltpu.get_barrier_semaphore()

    def in_group(d):
        return {"space": zed * GROUP + lax.rem(spot + d, GROUP)}

    def along_z(d):
        return {"space": lax.rem(zed + d, 2 * PAIRS) * GROUP + spot}

    def in_block(ds, dg):
        to = lax.rem(side + ds, 2), lax.rem(spot + dg, GROUP)
        return (2 * pair + to[0]) * GROUP + to[1], to[0] * GROUP + to[1]

    def along_dp(d):
        return {"dp": lax.rem(part + d, DP)}

    def tell(sem, peers):
        for peer in peers:
            pl.semaphore_signal(sem, inc=1, device_id=peer, device_id_type=MESH)

    across = [along_dp(d) for d in range(1, DP)]
    beside = [along_z(1), along_z(2 * PAIRS - 1)]
    near = [{"space": lax.rem(me + step, SPACE)} for step in NEAR]
    around = [in_group(d) for d in range(1, GROUP)]
    near += across + beside + around
    loads = [
        pltpu.make_async_copy(far, here, in_sems.at[n])
        for n, (far, here) in enumerate(
            (
                (occ, occ_v), (feat, feat_v), (wt, wt_v), (bias, bias_v), (cot, cot_v),
                (snd_in, snd), (nbr_in, nbr),
            )
        )
    ]
    for n in (0, 1, 2, 3, 5):
        loads[n].start()
    tell(barrier, near)

    constants = mask_parts()
    loads[0].wait()
    active = expand_mask(occ_v, cnt, *constants)
    mask[...] = active.astype(BF16)
    loads[1].wait()
    values = feat_v[...].astype(F32) * active
    for q in range(4):
        keep(src, flat, sides, q, values[:, 128 * q : 128 * q + 128])
    loads[5].wait()
    pack_faces(src, sides, snd, send_xy, send_z)

    for n in (4, 6):
        loads[n].start()
    pl.semaphore_wait(barrier, len(near))
    for copy in face_copies(send_xy, send_z, recv_xy, recv_z, sems):
        copy.start()
    for n in (2, 3):
        loads[n].wait()
    pack_weights(wt_v, bias_v, wsend)
    shares = [
        pltpu.make_async_remote_copy(
            src_ref=wsend,
            dst_ref=wall.at[part],
            send_sem=wsems.at[0],
            recv_sem=wsems.at[1],
            device_id=along_dp(d),
            device_id_type=MESH,
        )
        for d in range(1, DP)
    ]
    for copy in shares:
        copy.start()
    tell(ready.at[0], across + beside + around)
    wall[part] = wsend[...]
    own_faces(send_xy, send_z, recv_xy, recv_z)
    u_xy[0:8] = jnp.zeros((8, 8, LANES), F32)
    u_z[0:2] = jnp.zeros((2, 64, 128), F32)
    wait_bytes(wall.at[pl.ds(0, DP - 1)], wsems.at[0], wsems.at[1])
    build_bands(wall, both, forward, backward)
    bias_row = whole_bias(wall)
    wait_faces(recv_xy, recv_z, sems)
    pl.semaphore_wait(ready.at[0], len(across) + len(beside) + len(around))
    tell(ready.at[1], across + [along_z(2), along_z(2 * PAIRS - 2)])

    loads[6].wait()
    read_units(recv_xy, recv_z, u_xy, u_z)
    build_columns(src, nbr, u_xy, u_z, columns)
    loads[4].wait()
    bias_sum = jnp.zeros((1, 128), F32)
    for p in range(4):
        lanes = slice(128 * p, 128 * p + 128)
        pre = jnp.dot(
            columns[256 * p : 256 * p + 256, :], forward[...], preferred_element_type=F32
        )
        pre = pre + bias_row
        sig = jax.nn.sigmoid(pre)
        on = mask[:, lanes].astype(F32)
        block_out[:, lanes] = (pre * sig * on).astype(BF16)
        g = cot_v[:, lanes].astype(F32) * sig * (1.0 + pre * (1.0 - sig)) * on
        g = g.astype(BF16).astype(F32)
        keep(src, flat, sides, p, g)
        turned[:, 256 * p : 256 * p + 256] = g.T.astype(BF16)
        bias_sum += jnp.sum(g, axis=0, keepdims=True)
    pl.semaphore_wait(ready.at[1], len(across) + 2)
    tell(ready.at[2], [along_z(4), along_z(2 * PAIRS - 4)])

    low = low_half((16, 128))
    top_row = lax.broadcasted_iota(jnp.int32, (16, 128), 0) == 0
    bias_sum = bias_sum + swap_halves(bias_sum)
    bias_tile = jnp.where(top_row, jnp.broadcast_to(bias_sum, (16, 128)), 0.0)

    def reduce_copy(i, ds, dg):
        to, place = in_block(ds, dg)
        at = 2 * GROUP * lax.rem(i - part + DP, DP) + GROUP * ds + dg
        return pltpu.make_async_remote_copy(
            src_ref=packed.at[i, pl.ds(pl.multiple_of(place * PIECE, PIECE), PIECE)],
            dst_ref=rs_recv.at[at],
            send_sem=rs_sems.at[0],
            recv_sem=rs_sems.at[1],
            device_id={"space": to, "dp": i},
            device_id_type=MESH,
        )

    done = 0
    for owners, upto in (((0,), 3), ((1,), 5), ((2,), 7), ((3,), 9)):
        for t in range(done, upto):
            r = jnp.dot(
                turned[...], columns[:, 256 * t : 256 * t + 256], preferred_element_type=F32
            ).T
            r0, r1, r2, r3 = (r[64 * n : 64 * n + 64, :] for n in range(4))
            row = 192 * t
            sums[row : row + 64, :] = r3 + swap_halves(r0)
            sums[row + 64 : row + 128, :] = r0 + swap_halves(r1)
            sums[row + 128 : row + 192, :] = r1 + swap_halves(r2)
        done = upto
        for i in owners:
            for m in range(TILES):
                row = 16 * (27 * i + 2 * m)
                if m < TILES - 1:
                    other = swap_halves(sums[row + 16 : row + 32, :])
                else:
                    other = bias_tile
                tile = jnp.where(low, sums[row : row + 16, :], other)
                packed[i, 16 * m : 16 * m + 16, :] = tile.astype(BF16)
            packed[i, PACKED:PADDED, :] = jnp.zeros((PADDED - PACKED, 128), BF16)
        for i in owners:
            for ds, dg in BLOCK:
                reduce_copy(i, ds, dg).start()
    for d in range(1, DP):
        reduce_copy(lax.rem(part + d, DP), 0, 0).start()

    pack_faces(src, sides, snd, send_gxy, send_gz)
    own_faces(send_gxy, send_gz, recv_gxy, recv_gz)
    reduced = copies_of(rs_recv.at[pl.ds(1, 2 * DP * GROUP - 1)], rs_sems.at[0], rs_sems.at[1])
    reduced.wait_send()
    for copy in face_copies(send_gxy, send_gz, recv_gxy, recv_gz, gsems):
        copy.start()

    def grad_input(p):
        lanes = slice(128 * p, 128 * p + 128)
        r = lax.dot_general(
            columns[256 * p : 256 * p + 256, :],
            backward[...],
            (((1,), (1,)), ((), ())),
            preferred_element_type=F32,
        )
        grad_in[:, lanes] = (r * mask[:, lanes].astype(F32)).astype(BF16)

    reduced.wait_recv()
    mine = pl.ds(pl.multiple_of((side * GROUP + spot) * PIECE, PIECE), PIECE)
    total = packed[part, mine, :].astype(F32)
    for at in range(1, 2 * DP * GROUP):
        total += rs_recv[at].astype(F32)
    z_recv[pair] = total.astype(BF16)
    pl.semaphore_wait(ready.at[2], 2)
    for d in (4, 3, 5, 2, 6, 1, 7):
        pltpu.make_async_remote_copy(
            src_ref=z_recv.at[pair],
            dst_ref=z_recv.at[pair],
            send_sem=z_sems.at[0],
            recv_sem=z_sems.at[1],
            device_id={"space": (2 * lax.rem(pair + d, PAIRS) + side) * GROUP + spot},
            device_id_type=MESH,
        ).start()
    wait_faces(recv_gxy, recv_gz, gsems)
    read_units(recv_gxy, recv_gz, u_xy, u_z)
    build_columns(src, nbr, u_xy, u_z, columns)
    for p in range(4):
        grad_input(p)

    wait_bytes(z_recv.at[pl.ds(0, PAIRS - 1)], z_sems.at[0], z_sems.at[1])
    total = z_recv[0].astype(F32)
    for d in range(1, PAIRS):
        total += z_recv[d].astype(F32)
    full[mine, :] = total.astype(BF16)
    for ds, dg in BLOCK:
        pltpu.make_async_remote_copy(
            src_ref=full.at[mine],
            dst_ref=full.at[mine],
            send_sem=ag_sems.at[0],
            recv_sem=ag_sems.at[1],
            device_id={"space": in_block(ds, dg)[0]},
            device_id_type=MESH,
        ).start()
    wait_bytes(full.at[pl.ds(0, (2 * GROUP - 1) * PIECE)], ag_sems.at[0], ag_sems.at[1])


def last_kernel(block_in, grad_v, full, block_out, grad_out, gw, gb, rows):
    part = lax.axis_index("dp")
    block_out[...] = block_in[...]
    grad_out[...] = grad_v[...]
    for m in range(TILES):
        tile = full[16 * m : 16 * m + 16, :].astype(F32)
        other = swap_halves(tile)
        rows[32 * m : 32 * m + 16, :] = tile
        rows[32 * m + 16 : 32 * m + 32, :] = other
        if m == TILES - 1:
            picked = jnp.zeros((16, 128), F32)
            for i in range(DP):
                turn = pltpu.roll(other, 128 - 16 * i, axis=1) if i else other
                picked = jnp.where(part == i, turn, picked)
            gb[...] = picked[0:1, 0:16]
    for n in range(4):
        tile = rows[128 * n : 128 * n + 128, :].T[0:64, :]
        if n < 3:
            gw[:, 128 * n : 128 * n + 128] = tile
        else:
            gw[:, 384:432] = tile[:, 0:48]


def vmem(n):
    return [pl.BlockSpec(memory_space=pltpu.VMEM)] * n


def smem(n):
    return [pl.BlockSpec(memory_space=pltpu.SMEM)] * n


def of(shape, dtype):
    return jax.ShapeDtypeStruct(shape, dtype)


def body(features, occupancy, counts, send_units, neighbours, weight, conv_bias, cotangent):
    shard_shape = features.shape
    sends = send_units.transpose(0, 2, 1, 3).reshape(COLS, 1, 12)
    block_out, grad_in, full = pl.pallas_call(
        main_kernel,
        out_shape=(of((ROWS, LANES), BF16), of((ROWS, LANES), BF16), of((PADDED, 128), BF16)),
        in_specs=smem(1) + [pl.BlockSpec(memory_space=pltpu.HBM)] * 7,
        out_specs=tuple(vmem(3)),
        scratch_shapes=[
            pltpu.SMEM((COLS, 1, 12), jnp.int32),
            pltpu.SMEM((4, 26), jnp.int32),
            pltpu.VMEM((ROWS, LANES), BF16),
            pltpu.VMEM((4, LANES), jnp.int32),
            pltpu.VMEM((64, 432), BF16),
            pltpu.VMEM((1, 16), BF16),
            pltpu.VMEM((ROWS, LANES), BF16),
            pltpu.VMEM((ROWS, LANES), BF16),
            pltpu.VMEM((PACKED, 128), BF16),
            pltpu.VMEM((DP, PACKED, 128), BF16),
            pltpu.VMEM((4, 40, 8, 128), F32),
            pltpu.VMEM((48, 8, LANES), F32),
            pltpu.VMEM((12, 64, 128), F32),
            pltpu.VMEM((1024, WIDE), BF16),
            pltpu.VMEM((1728, 128), F32),
            pltpu.VMEM((WIDE, 128), BF16),
            pltpu.VMEM((128, WIDE), BF16),
            pltpu.VMEM((4, ROWS, 128), F32),
            pltpu.VMEM((10, 8, LANES), F32),
        ]
        + [pltpu.VMEM((COLS, 64, LANES), BF16), pltpu.VMEM((COLS, 128, 128), BF16)] * 4
        + [
            pltpu.VMEM((128, 1024), BF16),
            pltpu.VMEM((1728, 128), F32),
            pltpu.VMEM((DP, PADDED, 128), BF16),
            pltpu.VMEM((2 * DP * GROUP, PIECE, 128), BF16),
            pltpu.VMEM((PAIRS, PIECE, 128), BF16),
            pltpu.SemaphoreType.DMA((7,)),
            pltpu.SemaphoreType.DMA((2, 2)),
            pltpu.SemaphoreType.DMA((2, 2)),
            pltpu.SemaphoreType.DMA((2,)),
            pltpu.SemaphoreType.DMA((2,)),
            pltpu.SemaphoreType.DMA((2,)),
            pltpu.SemaphoreType.DMA((2,)),
            pltpu.SemaphoreType.REGULAR((3,)),
        ],
        compiler_params=pltpu.CompilerParams(
            collective_id=0, has_side_effects=True, vmem_limit_bytes=24 * 1024 * 1024
        ),
        name="main",
    )(
        counts,
        *(
            pltpu.with_memory_space_constraint(x, pltpu.HBM)
            for x in (
                features.reshape(ROWS, LANES), occupancy[0], weight.T, conv_bias.reshape(1, 16),
                cotangent.reshape(ROWS, LANES), sends, neighbours[0],
            )
        )
    )
    block_out, grad_in, gw, gb = pl.pallas_call(
        last_kernel,
        out_shape=(
            of((ROWS, LANES), BF16),
            of((ROWS, LANES), BF16),
            of((64, 432), F32),
            of((1, 16), F32),
        ),
        in_specs=vmem(3),
        out_specs=tuple(vmem(4)),
        scratch_shapes=[pltpu.VMEM((512, 128), F32)],
        compiler_params=pltpu.CompilerParams(vmem_limit_bytes=8 * 1024 * 1024),
        name="finish",
    )(block_out, grad_in, full)
    return block_out.reshape(shard_shape), grad_in.reshape(shard_shape), gw.T, gb.reshape(16)


def solution(mesh):
    placed = (
        P("dp", "space", None, None, None),
        P("dp", "space", None),
        P("dp", "space"),
        P("dp", "space", None, None),
        P("dp", "space", None),
        P("dp", None),
        P("dp"),
        P("dp", "space", None, None, None),
    )
    return jax.shard_map(
        body,
        mesh=mesh,
        in_specs=placed,
        out_specs=(
            P("dp", "space", None, None, None),
            P("dp", "space", None, None, None),
            P("dp", None),
            P("dp"),
        ),
        check_vma=False,
    )
```

```python
import jax
import jax.numpy as jnp
from jax import lax
from jax.experimental import pallas as pl
from jax.experimental.pallas import tpu as pltpu
from jax.sharding import PartitionSpec as P

F32 = jnp.float32
BF16 = jnp.bfloat16
MESH = pl.DeviceIdType.MESH
SPACE = 128
DP = 4
GROUP = 8
PAIRS = 8
COLS = 5
ROWS = 256
LANES = 512
WIDE = 2304
TILES = 14
PACKED = 224
PADDED = 256
PIECE = 16
NEAR = (1, 2, SPACE - 1, SPACE - 2)
BLOCK = [(ds, dg) for dg in (4, 5, 3, 2, 6, 7, 1, 0) for ds in (1, 0) if (ds, dg) != (0, 0)]
XY_LINKS = ((0, 1), (2, 3), (6, 7), (8, 9))


def low_half(shape):
    return lax.broadcasted_iota(jnp.int32, shape, len(shape) - 1) < 64


def near_column(step):
    return {1: 3, 2: 4, SPACE - 1: 1, SPACE - 2: 0}[step]


def swap_halves(v):
    return pltpu.roll(v, 64, axis=v.ndim - 1)


def keep(src, flat, sides, q, values):
    src[q, 0:8] = jnp.zeros((8, 8, 128), F32)
    src[q, 8:40] = values.reshape(32, 8, 128)
    flat[q] = values
    for y in range(2):
        sides[5 * y, :, 128 * q : 128 * q + 128] = jnp.zeros((8, 128), F32)
        for b in range(4):
            rows = pl.ds(64 * b + 7 * y, 8, stride=8)
            sides[5 * y + b + 1, :, 128 * q : 128 * q + 128] = flat[q, rows, :]


def pack_faces(src, sides, snd, out_xy, out_z):
    def slot_of(column, link):
        return ((snd[column, 0, link] + 6) * 43) >> 8

    def plane(column, link):
        slot = slot_of(column, link)
        face = link % 6
        if face >= 2:
            return sides[5 * (face - 2) + slot]
        return jnp.concatenate([src[q, slot * 8 + 7 * face] for q in range(4)], axis=1)

    low = low_half((64, 128))
    for column in range(COLS):
        for q, pair in enumerate(XY_LINKS):
            both = jnp.concatenate([plane(column, link) for link in pair], axis=0)
            out_xy[column, 16 * q : 16 * q + 16, :] = both.astype(BF16)
        for h in range(2):
            first = src[0, pl.ds(slot_of(column, 4 + 6 * h) * 8, 8)].reshape(64, 128)
            last = src[3, pl.ds(slot_of(column, 5 + 6 * h) * 8, 8)].reshape(64, 128)
            both = jnp.where(low, first, last)
            out_z[column, 64 * h : 64 * h + 64, :] = both.astype(BF16)


def face_copies(send_xy, send_z, recv_xy, recv_z, sems):
    me = lax.axis_index("space")
    copies = []
    for step in NEAR:
        column = near_column(step)
        for m, (src, dst) in enumerate(((send_xy, recv_xy), (send_z, recv_z))):
            copies.append(
                pltpu.make_async_remote_copy(
                    src_ref=src.at[column],
                    dst_ref=dst.at[column],
                    send_sem=sems.at[0, m],
                    recv_sem=sems.at[1, m],
                    device_id={"space": lax.rem(me + step, SPACE)},
                    device_id_type=MESH,
                )
            )
    return copies


def copies_of(view, send_sem, recv_sem):
    peer = lax.rem(lax.axis_index("space") + 1, SPACE)
    return pltpu.make_async_remote_copy(
        src_ref=view,
        dst_ref=view,
        send_sem=send_sem,
        recv_sem=recv_sem,
        device_id={"space": peer},
        device_id_type=MESH,
    )


def wait_bytes(view, send_sem, recv_sem):
    copies_of(view, send_sem, recv_sem).wait()


def wait_faces(recv_xy, recv_z, sems):
    wait_bytes(recv_xy.at[pl.ds(0, 4)], sems.at[0, 0], sems.at[1, 0])
    wait_bytes(recv_z.at[pl.ds(0, 4)], sems.at[0, 1], sems.at[1, 1])


def own_faces(send_xy, send_z, recv_xy, recv_z):
    recv_xy[2] = send_xy[2]
    recv_z[2] = send_z[2]


def pack_weights(wt, bias, wsend):
    row = jnp.concatenate([bias[...].astype(F32), jnp.zeros((1, 48), F32)], axis=1)
    first = lax.broadcasted_iota(jnp.int32, (16, 64), 0) == 0
    last = jnp.where(first, jnp.broadcast_to(row, (16, 64)), 0.0)
    for n in range(4):
        if n < 3:
            tile = wt[:, 128 * n : 128 * n + 128].astype(F32)
        else:
            tile = jnp.concatenate([wt[:, 384:432].astype(F32), jnp.zeros((64, 80), F32)], axis=1)
        tile = tile.T
        for m in range(4 if n < 3 else 2):
            other = tile[32 * m + 16 : 32 * m + 32] if 4 * n + m < TILES - 1 else last
            both = jnp.concatenate([tile[32 * m : 32 * m + 16], other], axis=1)
            wsend[64 * n + 16 * m : 64 * n + 16 * m + 16, :] = both.astype(BF16)


def mask_parts():
    place = lax.broadcasted_iota(jnp.int32, (64, LANES), 1)
    owner = (place >> 3) == lax.broadcasted_iota(jnp.int32, (64, LANES), 0)
    fold = lax.broadcasted_iota(jnp.int32, (LANES, 128), 0) & 7
    fold = (fold == lax.broadcasted_iota(jnp.int32, (LANES, 128), 1)).astype(F32).astype(BF16)
    widen = lax.broadcasted_iota(jnp.int32, (128, LANES), 1) >> 6
    widen = (widen == lax.broadcasted_iota(jnp.int32, (128, LANES), 0)).astype(F32).astype(BF16)
    return owner.astype(F32), fold, widen


def expand_mask(occ, cnt, owner, fold, widen):
    spread = []
    for b in range(4):
        live = jnp.minimum(jnp.maximum(cnt[0, 0] - b, 0), 1)
        row = (occ[b : b + 1, :] * live).astype(F32)
        spread.append(owner * jnp.broadcast_to(row, (64, LANES)))
    by_z = jnp.dot(jnp.concatenate(spread, axis=0).astype(BF16), fold, preferred_element_type=F32)
    return jnp.dot(by_z.astype(BF16), widen, preferred_element_type=F32)


def read_units(units_xy, units_z, u_xy, u_z):
    for column in range(COLS):
        planes = units_xy[column].astype(F32)
        u_xy[8 * column + 8 : 8 * column + 16] = planes.reshape(8, 8, LANES)
        planes = units_z[column].astype(F32)
        u_z[2 * column + 2 : 2 * column + 4] = planes.reshape(2, 64, 128)


def build_columns(src, nbr, u_xy, u_z, columns):
    low = low_half((8, 128))
    low_row = low_half((1, 128))
    depth = lax.broadcasted_iota(jnp.int32, (8, 640), 0)

    def one_brick(b, carry):
        where_of = {}
        for first in range(3):
            for second in range(3):
                for third in range(3):
                    o = (first - 1, second - 1, third - 1)
                    k = first * 9 + second * 3 + third
                    if k == 13:
                        continue
                    n = nbr[b, k if k < 13 else k - 1] + 12
                    column = (n * 171) >> 11
                    upper = (n - column * 12 + 2) >> 3
                    d = 0 if o[0] else 1 if o[1] else 2
                    face = 2 * d + (0 if o[d] == 1 else 1)
                    if d < 2:
                        where_of[o] = column * 8 + face + 4 * upper
                    else:
                        where_of[o] = column * 2 + upper

        def expand(c):
            t = [c[:, 128 * i : 128 * i + 128] for i in range(5)]
            return jnp.concatenate(
                [
                    t[0], jnp.where(low, t[1], t[4]),
                    t[1], jnp.where(low, t[2], t[0]),
                    t[2], jnp.where(low, t[3], t[1]),
                    t[3], jnp.where(low, t[4], t[2]),
                ],
                axis=1,
            )

        def side_row(ox, oy, row):
            rows = slice(row, row + 1)
            middle = u_xy[where_of[ox, oy, 0], rows, :]
            after = u_xy[where_of[ox, oy, 1], rows, 0:128]
            before = u_xy[where_of[ox, oy, -1], rows, 384:512]
            return jnp.concatenate([middle, jnp.where(low_row, after, before)], axis=1)

        for xx in range(10):
            if 1 <= xx <= 8:
                here = jnp.concatenate([src[q, b * 8 + 7 + xx] for q in range(4)], axis=1)
                rows = slice(8 * xx - 8, 8 * xx)
                after = u_z[where_of[0, 0, 1], rows, :]
                before = u_z[where_of[0, 0, -1], rows, :]
                lower, upper = side_row(0, -1, xx - 1), side_row(0, 1, xx - 1)
            else:
                ox = -1 if xx == 0 else 1
                here = u_xy[where_of[ox, 0, 0]]
                after = u_xy[where_of[ox, 0, 1], :, 0:128]
                before = u_xy[where_of[ox, 0, -1], :, 384:512]
                lower, upper = side_row(ox, -1, 7), side_row(ox, 1, 0)
            c = jnp.concatenate([here, jnp.where(low, after, before)], axis=1)
            down = jnp.where(depth == 0, jnp.broadcast_to(lower, (8, 640)), pltpu.roll(c, 1, axis=0))
            up = jnp.where(depth == 7, jnp.broadcast_to(upper, (8, 640)), pltpu.roll(c, 7, axis=0))
            tiles = [expand(tile) for tile in (down, c, up)]
            for e in range(3) if xx else ():
                pair = jnp.concatenate([before_tiles[e], tiles[e]], axis=0).astype(BF16)
                for a in range(3):
                    x = xx - 1 - a
                    if x not in (0, 2, 4, 6):
                        continue
                    lane = 256 * (3 * a + e)
                    for p in range(4):
                        rows = pl.ds(pl.multiple_of(b * 64, 64) + 256 * p + 8 * x, 16)
                        columns[rows, lane : lane + 256] = pair[:, 256 * p : 256 * p + 256]
            before_tiles = tiles
        return carry

    lax.fori_loop(0, 4, one_brick, 0, unroll=True)


def build_bands(wall, both, forward, backward):
    low = low_half((16, 128))
    for i in range(DP):
        for m in range(TILES):
            tile = wall[i, 16 * m : 16 * m + 16, :].astype(F32)
            turned = swap_halves(tile)
            row = 16 * (27 * i + 2 * m)
            both[row : row + 16, :] = jnp.where(low, tile, turned)
            if m < TILES - 1:
                both[row + 16 : row + 32, :] = jnp.where(low, turned, tile)
    low = low_half((64, 128))
    for t in range(9):
        w0, w1, w2 = (both[64 * (3 * t + f) : 64 * (3 * t + f) + 64, :] for f in range(3))
        parts = [
            jnp.where(low, w1, w0),
            jnp.where(low, w2, w1),
            jnp.where(low, 0.0, w2),
            jnp.where(low, w0, 0.0),
        ]
        for n, part in enumerate(parts):
            part = part.astype(BF16)
            row = 256 * t + 64 * n
            forward[row : row + 64, :] = part
            lane = 256 * (8 - t) + 128 * (n // 2)
            row = 64 * (n % 2)
            backward[row : row + 64, lane : lane + 128] = part


def whole_bias(wall):
    lane = lax.broadcasted_iota(jnp.int32, (16, 128), 1)
    total = jnp.zeros((16, 128), F32)
    for i in range(DP):
        tile = wall[i, PACKED - 16 : PACKED, :].astype(F32)
        tile = jnp.where((lane >= 64) & (lane < 80), tile, 0.0)
        total += pltpu.roll(tile, 64 + 16 * i, axis=1)
        total += pltpu.roll(tile, 16 * i, axis=1) if i else tile
    return total[0:1, :]


def main_kernel(
    cnt, feat, occ, wt, bias, cot, snd_in, nbr_in,
    block_out, grad_in, full,
    snd, nbr, feat_v, occ_v, wt_v, bias_v, cot_v, mask, wsend, wall,
    src, u_xy, u_z, columns, both, forward, backward,
    flat, sides, send_xy, send_z, recv_xy, recv_z, send_gxy, send_gz, recv_gxy, recv_gz, turned,
    sums, packed, rs_recv, z_recv,
    in_sems, sems, gsems, wsems, rs_sems, z_sems, ag_sems, ready,
):
    me, part = lax.axis_index("space"), lax.axis_index("dp")
    zed, spot = me // GROUP, lax.rem(me, GROUP)
    pair, side = zed // 2, lax.rem(zed, 2)
    barrier = pltpu.get_barrier_semaphore()

    def in_group(d):
        return {"space": zed * GROUP + lax.rem(spot + d, GROUP)}

    def along_z(d):
        return {"space": lax.rem(zed + d, 2 * PAIRS) * GROUP + spot}

    def in_block(ds, dg):
        to = lax.rem(side + ds, 2), lax.rem(spot + dg, GROUP)
        return (2 * pair + to[0]) * GROUP + to[1], to[0] * GROUP + to[1]

    def along_dp(d):
        return {"dp": lax.rem(part + d, DP)}

    def tell(sem, peers):
        for peer in peers:
            pl.semaphore_signal(sem, inc=1, device_id=peer, device_id_type=MESH)

    across = [along_dp(d) for d in range(1, DP)]
    beside = [along_z(1), along_z(2 * PAIRS - 1)]
    near = [{"space": lax.rem(me + step, SPACE)} for step in NEAR]
    around = [in_group(d) for d in range(1, GROUP)]
    near += across + beside + around
    loads = [
        pltpu.make_async_copy(far, here, in_sems.at[n])
        for n, (far, here) in enumerate(
            (
                (occ, occ_v), (feat, feat_v), (wt, wt_v), (bias, bias_v), (cot, cot_v),
                (snd_in, snd), (nbr_in, nbr),
            )
        )
    ]
    for n in (0, 1, 2, 3, 5):
        loads[n].start()
    tell(barrier, near)

    constants = mask_parts()
    loads[0].wait()
    active = expand_mask(occ_v, cnt, *constants)
    mask[...] = active.astype(BF16)
    loads[1].wait()
    values = feat_v[...].astype(F32) * active
    for q in range(4):
        keep(src, flat, sides, q, values[:, 128 * q : 128 * q + 128])
    loads[5].wait()
    pack_faces(src, sides, snd, send_xy, send_z)

    for n in (4, 6):
        loads[n].start()
    pl.semaphore_wait(barrier, len(near))
    for copy in face_copies(send_xy, send_z, recv_xy, recv_z, sems):
        copy.start()
    for n in (2, 3):
        loads[n].wait()
    pack_weights(wt_v, bias_v, wsend)
    shares = [
        pltpu.make_async_remote_copy(
            src_ref=wsend,
            dst_ref=wall.at[part],
            send_sem=wsems.at[0],
            recv_sem=wsems.at[1],
            device_id=along_dp(d),
            device_id_type=MESH,
        )
        for d in range(1, DP)
    ]
    for copy in shares:
        copy.start()
    tell(ready.at[0], across + beside + around)
    wall[part] = wsend[...]
    own_faces(send_xy, send_z, recv_xy, recv_z)
    u_xy[0:8] = jnp.zeros((8, 8, LANES), F32)
    u_z[0:2] = jnp.zeros((2, 64, 128), F32)
    wait_bytes(wall.at[pl.ds(0, DP - 1)], wsems.at[0], wsems.at[1])
    build_bands(wall, both, forward, backward)
    bias_row = whole_bias(wall)
    wait_faces(recv_xy, recv_z, sems)
    pl.semaphore_wait(ready.at[0], len(across) + len(beside) + len(around))
    tell(ready.at[1], across + [along_z(2), along_z(2 * PAIRS - 2)])

    loads[6].wait()
    read_units(recv_xy, recv_z, u_xy, u_z)
    build_columns(src, nbr, u_xy, u_z, columns)
    loads[4].wait()
    bias_sum = jnp.zeros((1, 128), F32)
    for p in range(4):
        lanes = slice(128 * p, 128 * p + 128)
        pre = jnp.dot(
            columns[256 * p : 256 * p + 256, :], forward[...], preferred_element_type=F32
        )
        pre = pre + bias_row
        sig = jax.nn.sigmoid(pre)
        on = mask[:, lanes].astype(F32)
        block_out[:, lanes] = (pre * sig * on).astype(BF16)
        g = cot_v[:, lanes].astype(F32) * sig * (1.0 + pre * (1.0 - sig)) * on
        g = g.astype(BF16).astype(F32)
        keep(src, flat, sides, p, g)
        turned[:, 256 * p : 256 * p + 256] = g.T.astype(BF16)
        bias_sum += jnp.sum(g, axis=0, keepdims=True)

    low = low_half((16, 128))
    top_row = lax.broadcasted_iota(jnp.int32, (16, 128), 0) == 0
    bias_sum = bias_sum + swap_halves(bias_sum)
    bias_tile = jnp.where(top_row, jnp.broadcast_to(bias_sum, (16, 128)), 0.0)

    def reduce_copy(i, ds, dg):
        to, place = in_block(ds, dg)
        at = 2 * GROUP * lax.rem(i - part + DP, DP) + GROUP * ds + dg
        return pltpu.make_async_remote_copy(
            src_ref=packed.at[i, pl.ds(pl.multiple_of(place * PIECE, PIECE), PIECE)],
            dst_ref=rs_recv.at[at],
            send_sem=rs_sems.at[0],
            recv_sem=rs_sems.at[1],
            device_id={"space": to, "dp": i},
            device_id_type=MESH,
        )

    done = 0
    for owners, upto in (((0,), 3), ((1,), 5), ((2,), 7), ((3,), 9)):
        for t in range(done, upto):
            r = jnp.dot(
                turned[...], columns[:, 256 * t : 256 * t + 256], preferred_element_type=F32
            ).T
            r0, r1, r2, r3 = (r[64 * n : 64 * n + 64, :] for n in range(4))
            row = 192 * t
            sums[row : row + 64, :] = r3 + swap_halves(r0)
            sums[row + 64 : row + 128, :] = r0 + swap_halves(r1)
            sums[row + 128 : row + 192, :] = r1 + swap_halves(r2)
        done = upto
        for i in owners:
            for m in range(TILES):
                row = 16 * (27 * i + 2 * m)
                if m < TILES - 1:
                    other = swap_halves(sums[row + 16 : row + 32, :])
                else:
                    other = bias_tile
                tile = jnp.where(low, sums[row : row + 16, :], other)
                packed[i, 16 * m : 16 * m + 16, :] = tile.astype(BF16)
            packed[i, PACKED:PADDED, :] = jnp.zeros((PADDED - PACKED, 128), BF16)
        if 0 in owners:
            pl.semaphore_wait(ready.at[1], len(across) + 2)
            tell(ready.at[2], [along_z(4), along_z(2 * PAIRS - 4)])
        for i in owners:
            for ds, dg in BLOCK:
                reduce_copy(i, ds, dg).start()
    for d in range(1, DP):
        reduce_copy(lax.rem(part + d, DP), 0, 0).start()

    pack_faces(src, sides, snd, send_gxy, send_gz)
    own_faces(send_gxy, send_gz, recv_gxy, recv_gz)
    reduced = copies_of(rs_recv.at[pl.ds(1, 2 * DP * GROUP - 1)], rs_sems.at[0], rs_sems.at[1])
    reduced.wait_send()
    for copy in face_copies(send_gxy, send_gz, recv_gxy, recv_gz, gsems):
        copy.start()

    def grad_input(p):
        lanes = slice(128 * p, 128 * p + 128)
        r = lax.dot_general(
            columns[256 * p : 256 * p + 256, :],
            backward[...],
            (((1,), (1,)), ((), ())),
            preferred_element_type=F32,
        )
        grad_in[:, lanes] = (r * mask[:, lanes].astype(F32)).astype(BF16)

    reduced.wait_recv()
    mine = pl.ds(pl.multiple_of((side * GROUP + spot) * PIECE, PIECE), PIECE)
    total = packed[part, mine, :].astype(F32)
    for at in range(1, 2 * DP * GROUP):
        total += rs_recv[at].astype(F32)
    z_recv[pair] = total.astype(BF16)
    pl.semaphore_wait(ready.at[2], 2)
    for d in (4, 3, 5, 2, 6, 1, 7):
        pltpu.make_async_remote_copy(
            src_ref=z_recv.at[pair],
            dst_ref=z_recv.at[pair],
            send_sem=z_sems.at[0],
            recv_sem=z_sems.at[1],
            device_id={"space": (2 * lax.rem(pair + d, PAIRS) + side) * GROUP + spot},
            device_id_type=MESH,
        ).start()
    wait_faces(recv_gxy, recv_gz, gsems)
    read_units(recv_gxy, recv_gz, u_xy, u_z)
    build_columns(src, nbr, u_xy, u_z, columns)
    for p in range(4):
        grad_input(p)

    wait_bytes(z_recv.at[pl.ds(0, PAIRS - 1)], z_sems.at[0], z_sems.at[1])
    total = z_recv[0].astype(F32)
    for d in range(1, PAIRS):
        total += z_recv[d].astype(F32)
    full[mine, :] = total.astype(BF16)
    for ds, dg in BLOCK:
        pltpu.make_async_remote_copy(
            src_ref=full.at[mine],
            dst_ref=full.at[mine],
            send_sem=ag_sems.at[0],
            recv_sem=ag_sems.at[1],
            device_id={"space": in_block(ds, dg)[0]},
            device_id_type=MESH,
        ).start()
    wait_bytes(full.at[pl.ds(0, (2 * GROUP - 1) * PIECE)], ag_sems.at[0], ag_sems.at[1])


def last_kernel(block_in, grad_v, full, block_out, grad_out, gw, gb, rows):
    part = lax.axis_index("dp")
    block_out[...] = block_in[...]
    grad_out[...] = grad_v[...]
    for m in range(TILES):
        tile = full[16 * m : 16 * m + 16, :].astype(F32)
        other = swap_halves(tile)
        rows[32 * m : 32 * m + 16, :] = tile
        rows[32 * m + 16 : 32 * m + 32, :] = other
        if m == TILES - 1:
            picked = jnp.zeros((16, 128), F32)
            for i in range(DP):
                turn = pltpu.roll(other, 128 - 16 * i, axis=1) if i else other
                picked = jnp.where(part == i, turn, picked)
            gb[...] = picked[0:1, 0:16]
    for n in range(4):
        tile = rows[128 * n : 128 * n + 128, :].T[0:64, :]
        if n < 3:
            gw[:, 128 * n : 128 * n + 128] = tile
        else:
            gw[:, 384:432] = tile[:, 0:48]


def vmem(n):
    return [pl.BlockSpec(memory_space=pltpu.VMEM)] * n


def smem(n):
    return [pl.BlockSpec(memory_space=pltpu.SMEM)] * n


def of(shape, dtype):
    return jax.ShapeDtypeStruct(shape, dtype)


def body(features, occupancy, counts, send_units, neighbours, weight, conv_bias, cotangent):
    shard_shape = features.shape
    sends = send_units.transpose(0, 2, 1, 3).reshape(COLS, 1, 12)
    block_out, grad_in, full = pl.pallas_call(
        main_kernel,
        out_shape=(of((ROWS, LANES), BF16), of((ROWS, LANES), BF16), of((PADDED, 128), BF16)),
        in_specs=smem(1) + [pl.BlockSpec(memory_space=pltpu.HBM)] * 7,
        out_specs=tuple(vmem(3)),
        scratch_shapes=[
            pltpu.SMEM((COLS, 1, 12), jnp.int32),
            pltpu.SMEM((4, 26), jnp.int32),
            pltpu.VMEM((ROWS, LANES), BF16),
            pltpu.VMEM((4, LANES), jnp.int32),
            pltpu.VMEM((64, 432), BF16),
            pltpu.VMEM((1, 16), BF16),
            pltpu.VMEM((ROWS, LANES), BF16),
            pltpu.VMEM((ROWS, LANES), BF16),
            pltpu.VMEM((PACKED, 128), BF16),
            pltpu.VMEM((DP, PACKED, 128), BF16),
            pltpu.VMEM((4, 40, 8, 128), F32),
            pltpu.VMEM((48, 8, LANES), F32),
            pltpu.VMEM((12, 64, 128), F32),
            pltpu.VMEM((1024, WIDE), BF16),
            pltpu.VMEM((1728, 128), F32),
            pltpu.VMEM((WIDE, 128), BF16),
            pltpu.VMEM((128, WIDE), BF16),
            pltpu.VMEM((4, ROWS, 128), F32),
            pltpu.VMEM((10, 8, LANES), F32),
        ]
        + [pltpu.VMEM((COLS, 64, LANES), BF16), pltpu.VMEM((COLS, 128, 128), BF16)] * 4
        + [
            pltpu.VMEM((128, 1024), BF16),
            pltpu.VMEM((1728, 128), F32),
            pltpu.VMEM((DP, PADDED, 128), BF16),
            pltpu.VMEM((2 * DP * GROUP, PIECE, 128), BF16),
            pltpu.VMEM((PAIRS, PIECE, 128), BF16),
            pltpu.SemaphoreType.DMA((7,)),
            pltpu.SemaphoreType.DMA((2, 2)),
            pltpu.SemaphoreType.DMA((2, 2)),
            pltpu.SemaphoreType.DMA((2,)),
            pltpu.SemaphoreType.DMA((2,)),
            pltpu.SemaphoreType.DMA((2,)),
            pltpu.SemaphoreType.DMA((2,)),
            pltpu.SemaphoreType.REGULAR((3,)),
        ],
        compiler_params=pltpu.CompilerParams(
            collective_id=0, has_side_effects=True, vmem_limit_bytes=24 * 1024 * 1024
        ),
        name="main",
    )(
        counts,
        *(
            pltpu.with_memory_space_constraint(x, pltpu.HBM)
            for x in (
                features.reshape(ROWS, LANES), occupancy[0], weight.T, conv_bias.reshape(1, 16),
                cotangent.reshape(ROWS, LANES), sends, neighbours[0],
            )
        )
    )
    block_out, grad_in, gw, gb = pl.pallas_call(
        last_kernel,
        out_shape=(
            of((ROWS, LANES), BF16),
            of((ROWS, LANES), BF16),
            of((64, 432), F32),
            of((1, 16), F32),
        ),
        in_specs=vmem(3),
        out_specs=tuple(vmem(4)),
        scratch_shapes=[pltpu.VMEM((512, 128), F32)],
        compiler_params=pltpu.CompilerParams(vmem_limit_bytes=8 * 1024 * 1024),
        name="finish",
    )(block_out, grad_in, full)
    return block_out.reshape(shard_shape), grad_in.reshape(shard_shape), gw.T, gb.reshape(16)


def solution(mesh):
    placed = (
        P("dp", "space", None, None, None),
        P("dp", "space", None),
        P("dp", "space"),
        P("dp", "space", None, None),
        P("dp", "space", None),
        P("dp", None),
        P("dp"),
        P("dp", "space", None, None, None),
    )
    return jax.shard_map(
        body,
        mesh=mesh,
        in_specs=placed,
        out_specs=(
            P("dp", "space", None, None, None),
            P("dp", "space", None, None, None),
            P("dp", None),
            P("dp"),
        ),
        check_vma=False,
    )
```
